512 devices in a mesh: tm: 32 (over z, core), col: 16 (over y, x).
Axes of the slice: x: 4, y: 4, z: 16, core: 2. Of those that a mesh axis runs over, the one named last changes fastest.
Arguments:
- diag_blocks: float32 [64, 768, 768], P('tm', 'col'), may hold values from -0.5 to 2, as said below
- left_blocks: float32 [32, 768, 768], P('tm', 'col'), may hold values from -1 to 0.5
- right_blocks: float32 [32, 768, 768], P('tm', 'col'), may hold values from -1 to 0.5
Outputs:
- blocks: float32 [64, 768, 768], P('tm', 'col')
- solved: float32 [32, 2, 768, 768], P('tm', None, 'col')
The draws below stay inside these ranges and needn't reach their ends.
Inputs may be any that keep to these rules, and one draw needn't show every extreme that they name: `diag_blocks`: every block is symmetric, and together with left_blocks, right_blocks and their transposes it forms a symmetric positive definite matrix.
All inputs are finite; a program needn't handle non-finite values.
Results may differ from the reference program's by a relative error of at most 0.00013.
Values sent between devices are 32-bit elements; how exact they have to be, the bound alone decides.
A program may use at most 64 MiB of HBM per device.

```python
import math
import jax
import jax.numpy as jnp
from jax import lax

B = 768
PAIRS = 32
NB = 64


def factor_parts(key):
    base_key = jax.random.fold_in(key, 7)
    diag_key, lag_key = jax.random.split(base_key)
    raw_diag = jax.random.uniform(diag_key, (NB, B, B), jnp.float32, -1.7320508, 1.7320508)
    raw_lag = jax.random.uniform(lag_key, (NB, B, B), jnp.float32, -1.7320508, 1.7320508)
    identity = jnp.eye(B, dtype=jnp.float32)
    diag_part = 0.85 * (identity + 0.8 * raw_diag / math.sqrt(B))
    lag_part = 0.5 * (identity + 0.22 * raw_lag / math.sqrt(B))
    return (diag_part, lag_part)


def cross_product(first_part, second_part):
    return jnp.einsum('kji,kjl->kil', first_part, second_part, precision=jax.lax.Precision.HIGHEST)


def draw_diag_blocks(key, part):
    diag_part, lag_part = factor_parts(key)
    lag_next = jnp.roll(lag_part, -1, axis=0)
    summed = cross_product(diag_part, diag_part) + cross_product(lag_next, lag_next)
    return 0.5 * (summed + jnp.swapaxes(summed, 1, 2))


def draw_left_blocks(key, part):
    diag_part, lag_part = factor_parts(key)
    return -cross_product(lag_part[1::2], diag_part[1::2])


def draw_right_blocks(key, part):
    diag_part, lag_part = factor_parts(key)
    diag_next = jnp.roll(diag_part, -1, axis=0)[1::2]
    lag_next = jnp.roll(lag_part, -1, axis=0)[1::2]
    return -cross_product(diag_next, lag_next)


def setup_inputs(seed: int = 0) -> dict:
    keys = jax.random.split(jax.random.key(seed), 4)
    diag_blocks = draw_diag_blocks(jax.random.fold_in(keys[3], 71), 0)
    left_blocks = draw_left_blocks(jax.random.fold_in(keys[3], 71), 0)
    right_blocks = draw_right_blocks(jax.random.fold_in(keys[3], 71), 0)
    return {"diag_blocks": diag_blocks, "left_blocks": left_blocks, "right_blocks": right_blocks}


def gram_cols(full_part, column_part):
    return lax.dot_general(full_part.astype(jnp.float32), column_part.astype(jnp.float32), (((0,), (0,)), ((), ())), precision=lax.Precision.HIGHEST, preferred_element_type=jnp.float32)

def lower_solve(factor, target):
    return lax.linalg.triangular_solve(factor, target, left_side=True, lower=True)

def first_level(operands):
    odd_block, left_part, right_part = operands
    factor = jnp.linalg.cholesky(odd_block)
    solved_left = lower_solve(factor, left_part)
    solved_right = lower_solve(factor, right_part)
    left_gram = gram_cols(solved_left, solved_left)
    right_gram = gram_cols(solved_right, solved_right)
    lower_next = -gram_cols(solved_right, solved_left)
    upper_next = -gram_cols(solved_left, solved_right)
    return (factor, solved_left, solved_right, left_gram, right_gram, lower_next, upper_next)

def second_level(operands):
    pivot_block, left_part, right_part = operands
    factor = jnp.linalg.cholesky(pivot_block)
    solved_left = lower_solve(factor, left_part)
    solved_right = lower_solve(factor, right_part)
    return (gram_cols(solved_left, solved_left), gram_cols(solved_right, solved_right))

def reference(diag_blocks, left_blocks, right_blocks):
    paired = diag_blocks.reshape(PAIRS, 2, B, B)
    left_cpl = jnp.swapaxes(left_blocks, 1, 2)
    right_cpl = jnp.swapaxes(right_blocks, 1, 2)
    factor_one, solved_left, solved_right, left_gram, right_gram, lower_next, upper_second = lax.map(first_level, (paired[:, 1], left_cpl, right_cpl))
    reduced = paired[:, 0] - left_gram - jnp.roll(right_gram, 1, axis=0)
    lower_second = jnp.roll(lower_next, 1, axis=0)
    first_gram, second_gram = lax.map(second_level, (reduced, lower_second, upper_second))
    final_block = reduced - jnp.roll(first_gram, -1, axis=0) - jnp.roll(second_gram, 1, axis=0)
    blocks = jnp.stack([final_block, factor_one], axis=1).reshape(2 * PAIRS, B, B)
    solved = jnp.stack([jnp.swapaxes(solved_left, 1, 2), jnp.swapaxes(solved_right, 1, 2)], axis=1)
    return (blocks, solved)
```

```python
import functools
import jax
import jax.numpy as jnp
from jax import lax
from jax.experimental import pallas as pl
from jax.experimental.pallas import tpu as pltpu
from jax.sharding import PartitionSpec as P

F32 = jnp.float32
BF16 = jnp.bfloat16
NT = 128
NN = (((1,), (0,)), ((), ()))
NTR = (((1,), (1,)), ((), ()))
TN = (((0,), (0,)), ((), ()))


def split(x):
    hi = x.astype(BF16)
    lo = (x - hi.astype(F32)).astype(BF16)
    return hi, lo


def bdot(a, b, dims):
    return lax.dot_general(a, b, dims, preferred_element_type=F32)


def dot3(a, b, dims):
    ah, al = a
    bh, bl = b
    return bdot(ah, bh, dims) + (bdot(ah, bl, dims) + bdot(al, bh, dims))


def lane(row, j):
    return jnp.broadcast_to(row[:, j:j + 1], (1, NT))


def factor_diag(d_ref, e_ref):
    row = lax.broadcasted_iota(jnp.int32, (NT, NT), 0)
    col = lax.broadcasted_iota(jnp.int32, (NT, NT), 1)
    e_ref[...] = jnp.where(row == col, 1.0, 0.0).astype(F32)
    us, es = None, None
    strips = NT // 8
    for s in range(strips):
        b = 8 * s
        d = [d_ref[b + i:b + i + 1, :] for i in range(8)]
        e = [e_ref[b + i:b + i + 1, :] for i in range(8)]
        p = {(i, j): lane(d[i], b + j) for i in range(8) for j in range(i + 1)}
        if us is not None:
            q = [[lane(us[k], b + i) for i in range(8)] for k in range(8)]
            for i in range(8):
                for j in range(i + 1):
                    acc = q[0][i] * q[0][j]
                    for k in range(1, 8):
                        acc = acc + q[k][i] * q[k][j]
                    p[i, j] = p[i, j] - acc
                acc_d = q[0][i] * us[0]
                acc_e = q[0][i] * es[0]
                for k in range(1, 8):
                    acc_d = acc_d + q[k][i] * us[k]
                    acc_e = acc_e + q[k][i] * es[k]
                d[i] = d[i] - acc_d
                e[i] = e[i] - acc_e
        for k in range(8):
            r = lax.rsqrt(p[k, k])
            d[k] = d[k] * r
            e[k] = e[k] * r
            for i in range(k + 1, 8):
                p[i, k] = p[i, k] * r
            for i in range(k + 1, 8):
                for j in range(k + 1, i + 1):
                    p[i, j] = p[i, j] - p[i, k] * p[j, k]
                d[i] = d[i] - p[i, k] * d[k]
                e[i] = e[i] - p[i, k] * e[k]
        us, es = d, e
        for i in range(8):
            d_ref[b + i:b + i + 1, :] = d[i]
            e_ref[b + i:b + i + 1, :] = e[i]
        if s + 2 < strips:
            lo_row = b + 16
            u8 = d_ref[b:b + 8, :]
            e8 = e_ref[b:b + 8, :]
            w = jnp.concatenate([u8, e8], axis=1)
            wh = w.astype(BF16).astype(F32)
            wl = w - wh
            rhs = jnp.concatenate([wh, wl, wh, wl], axis=0).astype(BF16)
            uh, ul = wh[:, :NT], wl[:, :NT]
            lhs = jnp.concatenate([uh, uh, ul, ul], axis=0).astype(BF16)
            upd = bdot(lhs, rhs, TN)[lo_row:, :]
            d_ref[lo_row:, :] = d_ref[lo_row:, :] - upd[:, :NT]
            e_ref[lo_row:, :] = e_ref[lo_row:, :] - upd[:, NT:]


MESH = pl.DeviceIdType.MESH


def reduce_block(blocks, a_ref, z_ref, linv_ref, d_ref, e_ref, keep_factor):
    size = blocks * NT
    rows = a_ref.shape[0]

    def step(j, carry):
        at = pl.ds(pl.multiple_of(j * NT, NT), NT)
        d_ref[...] = a_ref[at, at]
        factor_diag(d_ref, e_ref)
        linv_ref[j] = e_ref[...]
        if keep_factor:
            a_ref[at, at] = d_ref[...].T
        for i in range(blocks):

            @pl.when(j == i)
            def _():
                cols = slice(i * NT, (i + 1) * NT)
                below = (i + 1) * NT
                panel = dot3(split(a_ref[below:, cols]), split(e_ref[...]), NTR)
                a_ref[below:, cols] = panel
                ph, pw = split(panel)
                for k in range(i + 1, blocks):
                    r = k * NT
                    o = r - below
                    new = dot3((ph[o:], pw[o:]), (ph[o:o + NT], pw[o:o + NT]), NTR)
                    a_ref[r:, r:r + NT] = a_ref[r:, r:r + NT] - new

        return carry

    lax.fori_loop(0, blocks, step, 0)
    for i in reversed(range(blocks)):
        cols = slice(i * NT, (i + 1) * NT)
        below = (i + 1) * NT
        acc = a_ref[size:rows, cols]
        if below < size:
            acc = acc - dot3(split(z_ref[:, below:]), split(a_ref[below:size, cols]), NN)
        z_ref[:, cols] = dot3(split(acc), split(linv_ref[i]), NN)


def level_one(pivot, left, right, factor, solved, lgram, rgram, upper, mirror, a_ref, z_ref, linv_ref, d_ref, e_ref):
    size = pivot.shape[0]
    height = factor.shape[0]
    start = pl.multiple_of(lax.axis_index("col") * height, 16)
    mine = pl.ds(start, height)
    a_ref[:size, :] = pivot[...]
    a_ref[size:size + height, :] = left[mine, :]
    a_ref[size + height:, :] = right[mine, :]
    reduce_block(size // NT, a_ref, z_ref, linv_ref, d_ref, e_ref, True)
    row = start + lax.broadcasted_iota(jnp.int32, (height, size), 0)
    col = lax.broadcasted_iota(jnp.int32, (height, size), 1)
    factor[...] = jnp.where(col <= row, a_ref[mine, :], 0.0)
    solved[0] = a_ref[size:size + height, :]
    solved[1] = a_ref[size + height:, :]
    z = split(z_ref[...])
    for n in range(0, size, 256):
        cols = slice(n, n + 256)
        with_left = dot3(z, split(left[cols, :]), NTR)
        with_right = dot3(z, split(right[cols, :]), NTR)
        lgram[:, cols] = with_left[:height]
        mirror[:, cols] = -with_left[height:]
        upper[:, cols] = -with_right[:height]
        rgram[:, cols] = with_right[height:]


def level_two(pivot, first, second, fgram, sgram, a_ref, z_ref, linv_ref, d_ref, e_ref):
    size = pivot.shape[0]
    height = fgram.shape[0]
    mine = pl.ds(pl.multiple_of(lax.axis_index("col") * height, 16), height)
    a_ref[:size, :] = pivot[...]
    a_ref[size:size + height, :] = first[mine, :]
    a_ref[size + height:, :] = second[mine, :]
    reduce_block(size // NT, a_ref, z_ref, linv_ref, d_ref, e_ref, False)
    zf = split(z_ref[:height, :])
    zs = split(z_ref[height:, :])
    for n in range(0, size, 256):
        cols = slice(n, n + 256)
        fgram[:, cols] = dot3(zf, split(first[cols, :]), NTR)
        sgram[:, cols] = dot3(zs, split(second[cols, :]), NTR)


def ring(axis, by):
    return lax.rem(lax.axis_index(axis) + by, lax.axis_size(axis))


def enter(peers):
    barrier = pltpu.get_barrier_semaphore()
    for peer in peers:
        pl.semaphore_signal(barrier, inc=1, device_id=peer, device_id_type=MESH)
    pl.semaphore_wait(barrier, len(peers))


def to_all(src, full, send, recv, n, height):
    mine = pl.ds(lax.axis_index("col") * height, height)
    copies = []
    for by in range(1, n):
        copies.append(
            pltpu.make_async_remote_copy(
                src_ref=src,
                dst_ref=full.at[mine],
                send_sem=send.at[by],
                recv_sem=recv.at[by],
                device_id={"col": ring("col", by)},
                device_id_type=MESH,
            )
        )
    for copy in copies:
        copy.start()
    return copies


def gather_kernel(n, odd, left, right, odd_full, left_full, right_full, send, recv):
    height = odd.shape[0]
    enter([{"col": ring("col", by)} for by in range(1, n)])
    mine = pl.ds(pl.multiple_of(lax.axis_index("col") * height, 16), height)
    copies = []
    for i, (src, full) in enumerate(((odd, odd_full), (left, left_full), (right, right_full))):
        copies += to_all(src, full, send.at[i], recv.at[i], n, height)
    for src, full in ((odd, odd_full), (left, left_full), (right, right_full)):
        full[mine, :] = src[...]
    for copy in copies:
        copy.wait()


def next_kernel(n, t, even, lgram, rgram, upper, mirror, reduced, pivot, first, second, came, send, recv, tsend, trecv):
    height = even.shape[0]
    enter(
        [{"col": ring("col", by)} for by in range(1, n)]
        + [{"tm": ring("tm", 1)}, {"tm": ring("tm", t - 1)}]
    )
    mine = pl.ds(pl.multiple_of(lax.axis_index("col") * height, 16), height)

    def onward(i, src, dst):
        return pltpu.make_async_remote_copy(
            src_ref=src,
            dst_ref=dst,
            send_sem=tsend.at[i],
            recv_sem=trecv.at[i],
            device_id={"tm": ring("tm", 1)},
            device_id_type=MESH,
        )

    over_gram = onward(0, rgram, came)
    over_upper = onward(1, upper, first.at[mine])
    over_gram.start()
    over_upper.start()
    kept = even[...] - lgram[...]
    second[mine, :] = mirror[...]
    over_gram.wait_recv()
    kept = kept - came[...]
    reduced[...] = kept
    pivot[mine, :] = kept
    copies = to_all(reduced, pivot, send.at[0], recv.at[0], n, height)
    over_upper.wait_recv()
    copies += to_all(first.at[mine], first, send.at[1], recv.at[1], n, height)
    copies += to_all(mirror, second, send.at[2], recv.at[2], n, height)
    over_gram.wait_send()
    over_upper.wait_send()
    for copy in copies:
        copy.wait()


def last_kernel(t, reduced, fgram, sgram, final, came, send, recv):
    enter([{"tm": ring("tm", 1)}, {"tm": ring("tm", t - 1)}])
    copies = []
    for i, (src, by) in enumerate(((fgram, t - 1), (sgram, 1))):
        copies.append(
            pltpu.make_async_remote_copy(
                src_ref=src,
                dst_ref=came.at[i],
                send_sem=send.at[i],
                recv_sem=recv.at[i],
                device_id={"tm": ring("tm", by)},
                device_id_type=MESH,
            )
        )
    for copy in copies:
        copy.start()
    for copy in copies:
        copy.wait()
    final[...] = reduced[...] - came[0] - came[1]


def call(kernel, outs, scratch, remote, *args):
    side = {"collective_id": remote, "has_side_effects": True} if remote is not None else {}
    return pl.pallas_call(
        kernel,
        out_shape=[jax.ShapeDtypeStruct(s, F32) for s in outs],
        in_specs=[pl.BlockSpec(memory_space=pltpu.VMEM)] * len(args),
        out_specs=[pl.BlockSpec(memory_space=pltpu.VMEM)] * len(outs),
        scratch_shapes=scratch,
        compiler_params=pltpu.CompilerParams(vmem_limit_bytes=56 << 20, **side),
    )(*args)


def solution(mesh):
    n, t = mesh.shape["col"], mesh.shape["tm"]

    def shards(diag_blocks, left_blocks, right_blocks):
        even, odd = diag_blocks[0], diag_blocks[1]
        height, size = odd.shape
        part, full = (height, size), (size, size)
        sems = [pltpu.SemaphoreType.DMA((3, n))] * 2
        work = [
            pltpu.VMEM((size + 2 * height, size), F32),
            pltpu.VMEM((2 * height, size), F32),
            pltpu.VMEM((size // NT, NT, NT), F32),
            pltpu.VMEM((NT, NT), F32),
            pltpu.VMEM((NT, NT), F32),
        ]
        pivot, left, right = call(
            functools.partial(gather_kernel, n), [full] * 3, sems, 0, odd, left_blocks[0], right_blocks[0]
        )
        factor, solved, lgram, rgram, upper, mirror = call(
            level_one, [part, (2, *part)] + [part] * 4, work, None, pivot, left, right
        )
        two = [pltpu.SemaphoreType.DMA((2,))] * 2
        reduced, pivot, first, second = call(
            functools.partial(next_kernel, n, t),
            [part, full, full, full],
            [pltpu.VMEM(part, F32)] + sems + two,
            1,
            even,
            lgram,
            rgram,
            upper,
            mirror,
        )
        fgram, sgram = call(level_two, [part] * 2, work, None, pivot, first, second)
        (final,) = call(
            functools.partial(last_kernel, t), [part], [pltpu.VMEM((2, *part), F32)] + two, 2, reduced, fgram, sgram
        )
        return jnp.stack([final, factor]), solved[None]

    in_specs = (P("tm", "col", None), P("tm", "col", None), P("tm", "col", None))
    out_specs = (P("tm", "col", None), P("tm", None, "col", None))
    return jax.shard_map(shards, mesh=mesh, in_specs=in_specs, out_specs=out_specs, check_vma=False)
```

```python
import jax
import jax.numpy as jnp
from jax import lax
from jax.experimental import pallas as pl
from jax.experimental.pallas import tpu as pltpu
from jax.sharding import PartitionSpec as P

F32 = jnp.float32
BF16 = jnp.bfloat16
NT = 128
NN = (((1,), (0,)), ((), ()))
NTR = (((1,), (1,)), ((), ()))
TN = (((0,), (0,)), ((), ()))


def split(x):
    hi = x.astype(BF16)
    lo = (x - hi.astype(F32)).astype(BF16)
    return hi, lo


def bdot(a, b, dims):
    return lax.dot_general(a, b, dims, preferred_element_type=F32)


def dot3(a, b, dims):
    ah, al = a
    bh, bl = b
    return bdot(ah, bh, dims) + (bdot(ah, bl, dims) + bdot(al, bh, dims))


def lane(row, j):
    return jnp.broadcast_to(row[:, j:j + 1], (1, NT))


def factor_diag(d_ref, e_ref):
    row = lax.broadcasted_iota(jnp.int32, (NT, NT), 0)
    col = lax.broadcasted_iota(jnp.int32, (NT, NT), 1)
    e_ref[...] = jnp.where(row == col, 1.0, 0.0).astype(F32)
    us, es = None, None
    strips = NT // 8
    for s in range(strips):
        b = 8 * s
        d = [d_ref[b + i:b + i + 1, :] for i in range(8)]
        e = [e_ref[b + i:b + i + 1, :] for i in range(8)]
        p = {(i, j): lane(d[i], b + j) for i in range(8) for j in range(i + 1)}
        if us is not None:
            q = [[lane(us[k], b + i) for i in range(8)] for k in range(8)]
            for i in range(8):
                for j in range(i + 1):
                    acc = q[0][i] * q[0][j]
                    for k in range(1, 8):
                        acc = acc + q[k][i] * q[k][j]
                    p[i, j] = p[i, j] - acc
                acc_d = q[0][i] * us[0]
                acc_e = q[0][i] * es[0]
                for k in range(1, 8):
                    acc_d = acc_d + q[k][i] * us[k]
                    acc_e = acc_e + q[k][i] * es[k]
                d[i] = d[i] - acc_d
                e[i] = e[i] - acc_e
        for k in range(8):
            r = lax.rsqrt(p[k, k])
            d[k] = d[k] * r
            e[k] = e[k] * r
            for i in range(k + 1, 8):
                p[i, k] = p[i, k] * r
            for i in range(k + 1, 8):
                for j in range(k + 1, i + 1):
                    p[i, j] = p[i, j] - p[i, k] * p[j, k]
                d[i] = d[i] - p[i, k] * d[k]
                e[i] = e[i] - p[i, k] * e[k]
        us, es = d, e
        for i in range(8):
            d_ref[b + i:b + i + 1, :] = d[i]
            e_ref[b + i:b + i + 1, :] = e[i]
        if s + 2 < strips:
            lo_row = b + 16
            u8 = d_ref[b:b + 8, :]
            e8 = e_ref[b:b + 8, :]
            w = jnp.concatenate([u8, e8], axis=1)
            wh = w.astype(BF16).astype(F32)
            wl = w - wh
            rhs = jnp.concatenate([wh, wl, wh, wl], axis=0).astype(BF16)
            uh, ul = wh[:, :NT], wl[:, :NT]
            lhs = jnp.concatenate([uh, uh, ul, ul], axis=0).astype(BF16)
            upd = bdot(lhs, rhs, TN)[lo_row:, :]
            d_ref[lo_row:, :] = d_ref[lo_row:, :] - upd[:, :NT]
            e_ref[lo_row:, :] = e_ref[lo_row:, :] - upd[:, NT:]


MESH = pl.DeviceIdType.MESH


def reduce_block(blocks, a_ref, z_ref, linv_ref, d_ref, e_ref, keep_factor, during):
    size = blocks * NT
    rows = a_ref.shape[0]

    def step(j, carry):
        at = pl.ds(pl.multiple_of(j * NT, NT), NT)
        d_ref[...] = a_ref[at, at]
        factor_diag(d_ref, e_ref)
        linv_ref[j] = e_ref[...]
        if keep_factor:
            a_ref[at, at] = d_ref[...].T
        for i in range(blocks):

            @pl.when(j == i)
            def _():
                during(i)
                cols = slice(i * NT, (i + 1) * NT)
                below = (i + 1) * NT
                panel = dot3(split(a_ref[below:, cols]), split(e_ref[...]), NTR)
                a_ref[below:, cols] = panel
                ph, pw = split(panel)
                for k in range(i + 1, blocks):
                    r = k * NT
                    o = r - below
                    new = dot3((ph[o:], pw[o:]), (ph[o:o + NT], pw[o:o + NT]), NTR)
                    a_ref[r:, r:r + NT] = a_ref[r:, r:r + NT] - new

        return carry

    lax.fori_loop(0, blocks, step, 0)
    for i in reversed(range(blocks)):
        cols = slice(i * NT, (i + 1) * NT)
        below = (i + 1) * NT
        acc = a_ref[size:rows, cols]
        if below < size:
            acc = acc - dot3(split(z_ref[:, below:]), split(a_ref[below:size, cols]), NN)
        z_ref[:, cols] = dot3(split(acc), split(linv_ref[i]), NN)


def wrap(axis, by):
    size = lax.axis_size(axis)
    return lax.rem(lax.axis_index(axis) + (by + size), size)


def plus(a, b):
    return (a[0] + b[0], a[1] + b[1])


def times(k, a):
    return (k * a[0], k * a[1])


def torus_plan():
    whole, top, bottom = (0, 2), (0, 1), (1, 2)
    messages, rounds = [], []

    def leave(towards, block, rows, part):
        messages.append((towards, block, rows, part))
        return len(messages) - 1

    def relay(axis, block, part):
        return [
            leave(axis, plus(block, times(-1, axis)), top, part),
            leave(times(-1, axis), plus(block, axis), bottom, part),
        ]

    def both(axis, block, part):
        return [leave(axis, block, whole, part), leave(times(-1, axis), block, whole, part)]

    rings = ((0, 1), (1, 0))
    own = [m for axis in rings for m in both(axis, (0, 0), None)]
    rounds.append(([], own))
    far, sides, starts = [], [], []
    for part in range(2):
        a, b = rings[part], rings[1 - part]
        far.append(relay(a, (0, 0), part))
        sides.append([both(b, times(-1, a), part), both(b, a, part)])
        starts += far[part] + sides[part][0] + sides[part][1] + relay(b, (0, 0), part)
    rounds.append((own, starts))
    comes, starts, last = [], [], []
    for part in range(2):
        a, b = rings[part], rings[1 - part]
        comes += far[part] + sides[part][0] + sides[part][1]
        last.append(both(b, times(2, a), part))
        starts += last[part] + relay(b, times(-1, a), part) + relay(b, a, part)
    rounds.append((comes, starts))
    starts = []
    for part in range(2):
        a, b = rings[part], rings[1 - part]
        starts += relay(b, times(2, a), part)
    rounds.append((last[0] + last[1], starts))
    seen = {m for came, _ in rounds for m in came}
    rounds.append(([m for m in range(len(messages)) if m not in seen], []))
    return messages, rounds


MESSAGES, ROUNDS = torus_plan()
SIDE = 4


def gather_round(k, arrays):
    me = lax.axis_index("col")
    y, x = lax.div(me, SIDE), lax.rem(me, SIDE)

    def device(by):
        return lax.rem(y + (by[0] + SIDE), SIDE) * SIDE + lax.rem(x + (by[1] + SIDE), SIDE)

    def message(i, src, full, send, recv):
        towards, block, rows, part = MESSAGES[i]
        height, width = full.shape[0] // SIDE**2, full.shape[1]
        begin, length = rows[0] * height // 2, (rows[1] - rows[0]) * height // 2
        at = pl.ds(pl.multiple_of(device(block) * height + begin, 8), length)
        cols = pl.ds(0, width) if part is None else pl.ds(part * (width // 2), width // 2)
        there = full.at[at, cols]
        here = src if block == (0, 0) and part is None else there
        return pltpu.make_async_remote_copy(
            src_ref=here,
            dst_ref=there,
            send_sem=send.at[i],
            recv_sem=recv.at[i],
            device_id={"col": device(towards)},
            device_id_type=MESH,
        )

    comes, starts = ROUNDS[k]
    for array in arrays:
        for i in comes:
            message(i, *array).wait_recv()
    for array in arrays:
        for i in starts:
            message(i, *array).start()
    if k == len(ROUNDS) - 1:
        for array in arrays:
            for i in range(len(MESSAGES)):
                message(i, *array).wait_send()


def enter(others):
    me = lax.axis_index("col")
    y, x = lax.div(me, SIDE), lax.rem(me, SIDE)
    peers = [
        {"col": lax.rem(y + (dy + SIDE), SIDE) * SIDE + lax.rem(x + (dx + SIDE), SIDE)}
        for dy, dx in ((0, 1), (0, -1), (1, 0), (-1, 0))
    ] + others
    barrier = pltpu.get_barrier_semaphore()
    for peer in peers:
        pl.semaphore_signal(barrier, inc=1, device_id=peer, device_id_type=MESH)
    pl.semaphore_wait(barrier, len(peers))


def my_rows(height):
    return pl.ds(pl.multiple_of(lax.axis_index("col") * height, 16), height)


def level_one(diag, left, right, factor, solved, lgram, rgram, upper, mirror, *scratch):
    a_ref, z_ref, linv_ref, d_ref, e_ref, left_full, right_full, send, recv = scratch
    size = left_full.shape[0]
    height = factor.shape[0]
    mine = my_rows(height)
    enter([])
    pivot = [(diag.at[1], a_ref.at[pl.ds(0, size)], send.at[0], recv.at[0])]
    couplings = [
        (left, left_full, send.at[1], recv.at[1]),
        (right, right_full, send.at[2], recv.at[2]),
    ]
    gather_round(0, pivot)
    a_ref[mine, :] = diag[1]
    a_ref[size:size + height, :] = left[...]
    a_ref[size + height:, :] = right[...]
    left_full[mine, :] = left[...]
    right_full[mine, :] = right[...]
    for k in range(1, 4):
        gather_round(k, pivot)
    gather_round(0, couplings)
    gather_round(4, pivot)

    def during(j):
        if j < 3:
            gather_round(j + 1, couplings)

    reduce_block(size // NT, a_ref, z_ref, linv_ref, d_ref, e_ref, True, during)
    row = lax.axis_index("col") * height + lax.broadcasted_iota(jnp.int32, (height, size), 0)
    col = lax.broadcasted_iota(jnp.int32, (height, size), 1)
    factor[...] = jnp.where(col <= row, a_ref[mine, :], 0.0)
    solved[0] = a_ref[size:size + height, :]
    solved[1] = a_ref[size + height:, :]
    gather_round(4, couplings)
    z = split(z_ref[...])
    for n in range(0, size, 256):
        cols = slice(n, n + 256)
        with_left = dot3(z, split(left_full[cols, :]), NTR)
        with_right = dot3(z, split(right_full[cols, :]), NTR)
        lgram[:, cols] = with_left[:height]
        mirror[:, cols] = -with_left[height:]
        upper[:, cols] = -with_right[:height]
        rgram[:, cols] = with_right[height:]


def level_two(diag, factor, lgram, rgram, upper, mirror, blocks, *scratch):
    a_ref, z_ref, linv_ref, d_ref, e_ref, first, second, reduced, came, grams, send, recv, tsend, trecv = scratch
    size = first.shape[0]
    height = factor.shape[0]
    mine = my_rows(height)
    enter([{"tm": wrap("tm", 1)}, {"tm": wrap("tm", -1)}])

    def over(i, by, src, dst):
        return pltpu.make_async_remote_copy(
            src_ref=src,
            dst_ref=dst,
            send_sem=tsend.at[i],
            recv_sem=trecv.at[i],
            device_id={"tm": wrap("tm", by)},
            device_id_type=MESH,
        )

    over_gram = over(0, 1, rgram, came.at[0])
    over_upper = over(1, 1, upper, first.at[mine])
    over_gram.start()
    over_upper.start()
    kept = diag[0] - lgram[...]
    second[mine, :] = mirror[...]
    blocks[1] = factor[...]
    a_ref[size + height:, :] = mirror[...]
    over_gram.wait_recv()
    reduced[...] = kept - came[0]
    pivot = [(reduced, a_ref.at[pl.ds(0, size)], send.at[0], recv.at[0])]
    couplings = [
        (first.at[mine], first, send.at[1], recv.at[1]),
        (mirror, second, send.at[2], recv.at[2]),
    ]
    gather_round(0, pivot)
    a_ref[mine, :] = reduced[...]
    over_upper.wait_recv()
    a_ref[size:size + height, :] = first[mine, :]
    for k in range(1, 4):
        gather_round(k, pivot)
    gather_round(0, couplings)
    gather_round(4, pivot)

    def during(j):
        if j < 3:
            gather_round(j + 1, couplings)

    reduce_block(size // NT, a_ref, z_ref, linv_ref, d_ref, e_ref, False, during)
    gather_round(4, couplings)
    over_gram.wait_send()
    over_upper.wait_send()
    for i, full in enumerate((first, second)):
        z = split(z_ref[i * height:(i + 1) * height, :])
        for n in range(0, size, 256):
            cols = slice(n, n + 256)
            grams[i, :, cols] = dot3(z, split(full[cols, :]), NTR)
    back = [over(2, -1, grams.at[0], came.at[1]), over(3, 1, grams.at[1], came.at[2])]
    for copy in back:
        copy.start()
    for copy in back:
        copy.wait()
    blocks[0] = reduced[...] - came[1] - came[2]


def call(kernel, outs, scratch, collective, *args):
    return pl.pallas_call(
        kernel,
        out_shape=[jax.ShapeDtypeStruct(s, F32) for s in outs],
        in_specs=[pl.BlockSpec(memory_space=pltpu.VMEM)] * len(args),
        out_specs=[pl.BlockSpec(memory_space=pltpu.VMEM)] * len(outs),
        scratch_shapes=scratch,
        compiler_params=pltpu.CompilerParams(
            vmem_limit_bytes=56 << 20, collective_id=collective, has_side_effects=True
        ),
    )(*args)


def solution(mesh):
    def shards(diag_blocks, left_blocks, right_blocks):
        height, size = left_blocks.shape[1:]
        part, full = (height, size), (size, size)
        sems = [pltpu.SemaphoreType.DMA((3, len(MESSAGES)))] * 2
        work = [
            pltpu.VMEM((size + 2 * height, size), F32),
            pltpu.VMEM((2 * height, size), F32),
            pltpu.VMEM((size // NT, NT, NT), F32),
            pltpu.VMEM((NT, NT), F32),
            pltpu.VMEM((NT, NT), F32),
            pltpu.VMEM(full, F32),
            pltpu.VMEM(full, F32),
        ]
        factor, solved, *rows = call(
            level_one,
            [part, (2, *part)] + [part] * 4,
            work + sems,
            0,
            diag_blocks,
            left_blocks[0],
            right_blocks[0],
        )
        extra = [pltpu.VMEM(part, F32), pltpu.VMEM((3, *part), F32), pltpu.VMEM((2, *part), F32)]
        over = [pltpu.SemaphoreType.DMA((4,))] * 2
        (blocks,) = call(
            level_two, [(2, *part)], work + extra + sems + over, 1, diag_blocks, factor, *rows
        )
        return blocks, solved[None]

    in_specs = (P("tm", "col", None), P("tm", "col", None), P("tm", "col", None))
    out_specs = (P("tm", "col", None), P("tm", None, "col", None))
    return jax.shard_map(shards, mesh=mesh, in_specs=in_specs, out_specs=out_specs, check_vma=False)
```

```python
import jax
import jax.numpy as jnp
from jax import lax
from jax.experimental import pallas as pl
from jax.experimental.pallas import tpu as pltpu
from jax.sharding import PartitionSpec as P

F32 = jnp.float32
BF16 = jnp.bfloat16
NT = 128
SIDE = 4
MESH = pl.DeviceIdType.MESH
NN = (((1,), (0,)), ((), ()))
NTR = (((1,), (1,)), ((), ()))
TN = (((0,), (0,)), ((), ()))


def split(x):
    hi = x.astype(BF16)
    lo = (x - hi.astype(F32)).astype(BF16)
    return hi, lo


def bdot(a, b, dims):
    return lax.dot_general(a, b, dims, preferred_element_type=F32)


def dot3(a, b, dims):
    ah, al = a
    bh, bl = b
    return bdot(ah, bh, dims) + (bdot(ah, bl, dims) + bdot(al, bh, dims))


def lane(rows, j):
    return jnp.broadcast_to(rows[:, j:j + 1], (8, NT))

def factor_diag(d_ref, e_ref, p_ref):
    row = lax.broadcasted_iota(jnp.int32, (NT, NT), 0)
    col = lax.broadcasted_iota(jnp.int32, (NT, NT), 1)
    e_ref[...] = jnp.where(row == col, 1.0, 0.0).astype(F32)
    strips = NT // 8
    for s in range(strips):
        b = 8 * s
        half = 64 * (s % 2)
        strip = d_ref[b:b + 8, :]
        for j in range(8):
            p_ref[half + 8 * j:half + 8 * j + 8, :] = lane(strip, b + j)
        p = {(i, j): p_ref[pl.ds(half + 8 * j + i, 8, stride=0), :] for i in range(8) for j in range(i + 1)}
        d = [d_ref[pl.ds(b + i, 8, stride=0), :] for i in range(8)]
        e = [e_ref[pl.ds(b + i, 8, stride=0), :] for i in range(8)]
        more = s + 1 < strips
        if more:
            nd = d_ref[b + 8:b + 16, :]
            ne = e_ref[b + 8:b + 16, :]
            t = [lane(nd, b + k) for k in range(8)]
        for k in range(8):
            r = lax.rsqrt(p[k, k])
            for i in range(k + 1, 8):
                p[i, k] = p[i, k] * r
            for i in range(k + 1, 8):
                for j in range(k + 1, i + 1):
                    p[i, j] = p[i, j] - p[i, k] * p[j, k]
            d[k] = d[k] * r
            e[k] = e[k] * r
            for i in range(k + 1, 8):
                d[i] = d[i] - p[i, k] * d[k]
                e[i] = e[i] - p[i, k] * e[k]
            d_ref[b + k:b + k + 1, :] = d[k][:1]
            e_ref[b + k:b + k + 1, :] = e[k][:1]
            if more:
                t[k] = t[k] * r
                for i in range(k + 1, 8):
                    t[i] = t[i] - p[i, k] * t[k]
                nd = nd - t[k] * d[k]
                ne = ne - t[k] * e[k]
        if more:
            d_ref[b + 8:b + 16, :] = nd
            e_ref[b + 8:b + 16, :] = ne
        if s + 2 < strips:
            lo_row = b + 16
            w = jnp.concatenate([d_ref[b:b + 8, :], e_ref[b:b + 8, :]], axis=1)
            wh = w.astype(BF16).astype(F32)
            wl = w - wh
            rhs = jnp.concatenate([wh, wl, wh, wl], axis=0).astype(BF16)
            uh, ul = wh[:, :NT], wl[:, :NT]
            lhs = jnp.concatenate([uh, uh, ul, ul], axis=0).astype(BF16)
            upd = bdot(lhs, rhs, TN)[lo_row:, :]
            d_ref[lo_row:, :] = d_ref[lo_row:, :] - upd[:, :NT]
            e_ref[lo_row:, :] = e_ref[lo_row:, :] - upd[:, NT:]


def reduce_block(a_ref, z_ref, linv_ref, d_ref, e_ref, p_ref, keep_factor, during):
    size = a_ref.shape[1]
    blocks = size // NT
    rows = a_ref.shape[0]

    def step(j, carry):
        at = pl.ds(pl.multiple_of(j * NT, NT), NT)
        d_ref[...] = a_ref[at, at]
        factor_diag(d_ref, e_ref, p_ref)
        linv_ref[j] = e_ref[...]
        if keep_factor:
            a_ref[at, at] = d_ref[...].T
        for i in range(blocks):

            @pl.when(j == i)
            def _():
                during(i)
                cols = slice(i * NT, (i + 1) * NT)
                below = (i + 1) * NT
                panel = dot3(split(a_ref[below:, cols]), split(e_ref[...]), NTR)
                a_ref[below:, cols] = panel
                ph, pw = split(a_ref[below:, :below] if i == 1 else panel)
                for k in range(i + 1, 2 if i == 0 else blocks):
                    r = k * NT
                    o = r - below
                    new = dot3((ph[o:], pw[o:]), (ph[o:o + NT], pw[o:o + NT]), NTR)
                    a_ref[r:, r:r + NT] = a_ref[r:, r:r + NT] - new

        return carry

    lax.fori_loop(0, blocks, step, 0)
    for i in reversed(range(blocks)):
        cols = slice(i * NT, (i + 1) * NT)
        below = (i + 1) * NT
        acc = a_ref[size:rows, cols]
        if below < size:
            acc = acc - dot3(split(z_ref[:, below:]), split(a_ref[below:size, cols]), NN)
        z_ref[:, cols] = dot3(split(acc), split(linv_ref[i]), NN)


def wrap(axis, by):
    size = lax.axis_size(axis)
    return lax.rem(lax.axis_index(axis) + (by + size), size)


def plus(a, b):
    return (a[0] + b[0], a[1] + b[1])


def times(k, a):
    return (k * a[0], k * a[1])


RINGS = ((0, 1), (1, 0))
WHOLE, TOP, BOTTOM = (0, 2), (0, 1), (1, 2)


def relay_plan():
    messages, rounds = [], []

    def leave(towards, block, rows, part):
        messages.append((towards, block, rows, part))
        return len(messages) - 1

    def relay(axis, block, part):
        return [
            leave(axis, plus(block, times(-1, axis)), TOP, part),
            leave(times(-1, axis), plus(block, axis), BOTTOM, part),
        ]

    def both(axis, block, part):
        return [leave(axis, block, WHOLE, part), leave(times(-1, axis), block, WHOLE, part)]

    own = [m for axis in RINGS for m in both(axis, (0, 0), None)]
    rounds.append(([], own))
    far, sides, starts = [], [], []
    for part in range(2):
        a, b = RINGS[part], RINGS[1 - part]
        far.append(relay(a, (0, 0), part))
        sides.append([both(b, times(-1, a), part), both(b, a, part)])
        starts += far[part] + sides[part][0] + sides[part][1] + relay(b, (0, 0), part)
    rounds.append((own, starts))
    comes, starts, last = [], [], []
    for part in range(2):
        a, b = RINGS[part], RINGS[1 - part]
        comes += far[part] + sides[part][0] + sides[part][1]
        last.append(both(b, times(2, a), part))
        starts += last[part] + relay(b, times(-1, a), part) + relay(b, a, part)
    rounds.append((comes, starts))
    starts = []
    for part in range(2):
        a, b = RINGS[part], RINGS[1 - part]
        starts += relay(b, times(2, a), part)
    rounds.append((last[0] + last[1], starts))
    seen = {m for came, _ in rounds for m in came}
    rounds.append(([m for m in range(len(messages)) if m not in seen], []))
    return messages, rounds


def direct_plan():
    messages, starts = [], []
    hops = [[axis, times(-1, axis), times(2, axis)] for axis in RINGS]
    for ring in hops:
        for hop in ring:
            messages.append((hop, (0, 0), WHOLE, None))
    own = list(range(len(messages)))
    for part in range(2):
        for hop in hops[part]:
            for onward in hops[1 - part]:
                starts.append(len(messages))
                messages.append((onward, times(-1, hop), WHOLE, part))
    return messages, [([], own), (own, starts), (starts, [])]


RELAY, DIRECT = relay_plan(), direct_plan()
SLOTS = max(len(RELAY[0]), len(DIRECT[0]))


def col_device(by):
    me = lax.axis_index("col")
    y, x = lax.div(me, SIDE), lax.rem(me, SIDE)
    return lax.rem(y + (by[0] + SIDE), SIDE) * SIDE + lax.rem(x + (by[1] + SIDE), SIDE)


def gather_round(plan, k, *arrays):
    messages, rounds = plan

    def message(i, src, full, cols, send, recv):
        towards, block, rows, part = messages[i]
        height = full.shape[0] // SIDE**2
        begin, length = rows[0] * height // 2, (rows[1] - rows[0]) * height // 2
        at = pl.ds(pl.multiple_of(col_device(block) * height + begin, 8), length)
        half = (cols[1] - cols[0]) // 2
        over = pl.ds(*((cols[0], 2 * half) if part is None else (cols[0] + part * half, half)))
        there = full.at[at, over]
        return pltpu.make_async_remote_copy(
            src_ref=src.at[:, over] if block == (0, 0) and part is None else there,
            dst_ref=there,
            send_sem=send.at[i],
            recv_sem=recv.at[i],
            device_id={"col": col_device(towards)},
            device_id_type=MESH,
        )

    comes, starts = rounds[k]
    for array in arrays:
        for i in comes:
            message(i, *array).wait_recv()
    for array in arrays:
        for i in starts:
            message(i, *array).start()
    if k == len(rounds) - 1:
        for array in arrays:
            for i in range(len(messages)):
                message(i, *array).wait_send()


def enter(others):
    peers = [{"col": col_device(times(k, axis))} for axis in RINGS for k in (1, -1, 2)] + others
    barrier = pltpu.get_barrier_semaphore()
    for peer in peers:
        pl.semaphore_signal(barrier, inc=1, device_id=peer, device_id_type=MESH)
    pl.semaphore_wait(barrier, len(peers))


def kernel(diag, left, right, blocks, solved, *scratch):
    (a_one, a_two, left_full, right_full, first, second, z_ref, linv_ref, d_ref, e_ref, p_ref) = scratch[:11]
    (lgram, rgram, upper, mirror, reduced, came, grams, send, recv, tsend, trecv) = scratch[11:]
    height, size = left.shape
    near, rest = (0, 2 * NT), (2 * NT, size)
    mine = pl.ds(pl.multiple_of(lax.axis_index("col") * height, 16), height)
    enter([{"tm": wrap("tm", 1)}, {"tm": wrap("tm", -1)}])

    def factor(level, a_ref, pivot_rows, first_rows, second_rows, first_full, second_full, ready):
        full = a_ref.at[pl.ds(0, size)]
        sems = [(send.at[level, i], recv.at[level, i]) for i in range(4)]
        head = (pivot_rows, full, near, *sems[0])
        tail = (pivot_rows, full, rest, *sems[1])
        couplings = [
            (first_rows, first_full, (0, size), *sems[2]),
            (second_rows, second_full, (0, size), *sems[3]),
        ]
        gather_round(DIRECT, 1, head)
        a_ref[mine, :] = pivot_rows[...]
        ready()
        gather_round(DIRECT, 1, tail)
        gather_round(RELAY, 0, *couplings)
        gather_round(DIRECT, 2, head)

        def during(j):
            if j == 1:
                gather_round(DIRECT, 2, tail)
            if j < 3:
                gather_round(RELAY, j + 1, *couplings)

        reduce_block(a_ref, z_ref, linv_ref, d_ref, e_ref, p_ref, level == 0, during)
        gather_round(RELAY, 4, *couplings)

    def begin(level, a_ref, pivot_rows, cols):
        i = 0 if cols == near else 1
        gather_round(
            DIRECT, 0, (pivot_rows, a_ref.at[pl.ds(0, size)], cols, send.at[level, i], recv.at[level, i])
        )

    def over(i, by, src, dst):
        return pltpu.make_async_remote_copy(
            src_ref=src,
            dst_ref=dst,
            send_sem=tsend.at[i],
            recv_sem=trecv.at[i],
            device_id={"tm": wrap("tm", by)},
            device_id_type=MESH,
        )

    odd = diag.at[1]
    begin(0, a_one, odd, near)
    begin(0, a_one, odd, rest)

    def ready_one():
        a_one[size:size + height, :] = left[...]
        a_one[size + height:, :] = right[...]
        left_full[mine, :] = left[...]
        right_full[mine, :] = right[...]

    factor(0, a_one, odd, left, right, left_full, right_full, ready_one)

    z = split(z_ref[...])
    head_gram = over(0, 1, rgram.at[:, pl.ds(0, 2 * NT)], came.at[0, :, pl.ds(0, 2 * NT)])
    tail_gram = over(1, 1, rgram.at[:, pl.ds(2 * NT, size - 2 * NT)], came.at[0, :, pl.ds(2 * NT, size - 2 * NT)])
    over_upper = over(2, 1, upper, first.at[mine])

    def with_right(cols):
        both = dot3(z, split(right_full[cols, :]), NTR)
        upper[:, cols] = -both[:height]
        rgram[:, cols] = both[height:]

    def with_left(cols):
        both = dot3(z, split(left_full[cols, :]), NTR)
        lgram[:, cols] = both[:height]
        mirror[:, cols] = -both[height:]

    parts = [slice(n, n + 2 * NT) for n in range(0, size, 2 * NT)]
    with_right(parts[0])
    head_gram.start()
    for cols in parts[1:]:
        with_right(cols)
    tail_gram.start()
    over_upper.start()
    with_left(parts[0])
    head_gram.wait_recv()
    reduced[:, parts[0]] = diag[0, :, parts[0]] - lgram[:, parts[0]] - came[0, :, parts[0]]
    begin(1, a_two, reduced, near)
    for cols in parts[1:]:
        with_left(cols)
    tail_gram.wait_recv()
    reduced[:, 2 * NT:] = diag[0, :, 2 * NT:] - lgram[:, 2 * NT:] - came[0, :, 2 * NT:]
    begin(1, a_two, reduced, rest)
    row = lax.axis_index("col") * height + lax.broadcasted_iota(jnp.int32, (height, size), 0)
    col = lax.broadcasted_iota(jnp.int32, (height, size), 1)
    blocks[1] = jnp.where(col <= row, a_one[mine, :], 0.0)
    solved[0] = a_one[size:size + height, :]
    solved[1] = a_one[size + height:, :]

    def ready_two():
        second[mine, :] = mirror[...]
        a_two[size + height:, :] = mirror[...]
        over_upper.wait_recv()
        a_two[size:size + height, :] = first[mine, :]

    factor(1, a_two, reduced, first.at[mine], mirror, first, second, ready_two)

    zs = [split(z_ref[i * height:(i + 1) * height, :]) for i in range(2)]
    back = []
    for n, cols in enumerate(parts):
        there = pl.ds(n * 2 * NT, 2 * NT)
        for i, (full, by) in enumerate(((first, -1), (second, 1))):
            grams[i, :, cols] = dot3(zs[i], split(full[cols, :]), NTR)
            back.append(over(3 + 2 * n + i, by, grams.at[i, :, there], came.at[1 + i, :, there]))
            back[-1].start()
    for copy in (head_gram, tail_gram, over_upper):
        copy.wait_send()
    for copy in back:
        copy.wait()
    blocks[0] = reduced[...] - came[1] - came[2]


def solution(mesh):
    def shards(diag_blocks, left_blocks, right_blocks):
        height, size = left_blocks.shape[1:]
        part, full = (height, size), (size, size)
        tall = (size + 2 * height, size)
        shapes = [tall, tall, full, full, full, full, (2 * height, size), (size // NT, NT, NT)]
        shapes += [(NT, NT)] * 3 + [part] * 5 + [(3, *part), (2, *part)]
        sems = [pltpu.SemaphoreType.DMA((2, 4, SLOTS))] * 2 + [pltpu.SemaphoreType.DMA((16,))] * 2
        blocks, solved = pl.pallas_call(
            kernel,
            out_shape=[jax.ShapeDtypeStruct((2, *part), F32)] * 2,
            in_specs=[pl.BlockSpec(memory_space=pltpu.VMEM)] * 3,
            out_specs=[pl.BlockSpec(memory_space=pltpu.VMEM)] * 2,
            scratch_shapes=[pltpu.VMEM(s, F32) for s in shapes] + sems,
            compiler_params=pltpu.CompilerParams(
                vmem_limit_bytes=56 << 20, collective_id=0, has_side_effects=True
            ),
        )(diag_blocks, left_blocks[0], right_blocks[0])
        return blocks, solved[None]

    in_specs = (P("tm", "col", None), P("tm", "col", None), P("tm", "col", None))
    out_specs = (P("tm", "col", None), P("tm", None, "col", None))
    return jax.shard_map(shards, mesh=mesh, in_specs=in_specs, out_specs=out_specs, check_vma=False)
```

```python
import jax
import jax.numpy as jnp
from jax import lax
from jax.experimental import pallas as pl
from jax.experimental.pallas import tpu as pltpu
from jax.sharding import PartitionSpec as P

F32 = jnp.float32
BF16 = jnp.bfloat16
NT = 128
SIDE = 4
MESH = pl.DeviceIdType.MESH
NN = (((1,), (0,)), ((), ()))
NTR = (((1,), (1,)), ((), ()))
TN = (((0,), (0,)), ((), ()))


def split(x):
    hi = x.astype(BF16)
    lo = (x - hi.astype(F32)).astype(BF16)
    return hi, lo


def bdot(a, b, dims):
    return lax.dot_general(a, b, dims, preferred_element_type=F32)


def dot3(a, b, dims):
    ah, al = a
    bh, bl = b
    return bdot(ah, bh, dims) + (bdot(ah, bl, dims) + bdot(al, bh, dims))


def lane(rows, j):
    return jnp.broadcast_to(rows[:, j:j + 1], (8, NT))

def factor_diag(d_ref, e_ref, p_ref):
    row = lax.broadcasted_iota(jnp.int32, (NT, NT), 0)
    col = lax.broadcasted_iota(jnp.int32, (NT, NT), 1)
    e_ref[...] = jnp.where(row == col, 1.0, 0.0).astype(F32)
    strips = NT // 8
    for s in range(strips):
        b = 8 * s
        half = 64 * (s % 2)
        strip = d_ref[b:b + 8, :]
        for j in range(8):
            p_ref[half + 8 * j:half + 8 * j + 8, :] = lane(strip, b + j)
        p = {(i, j): p_ref[pl.ds(half + 8 * j + i, 8, stride=0), :] for i in range(8) for j in range(i + 1)}
        d = [d_ref[pl.ds(b + i, 8, stride=0), :] for i in range(8)]
        e = [e_ref[pl.ds(b + i, 8, stride=0), :] for i in range(8)]
        more = s + 1 < strips
        if more:
            nd = d_ref[b + 8:b + 16, :]
            ne = e_ref[b + 8:b + 16, :]
            t = [lane(nd, b + k) for k in range(8)]
        for k in range(8):
            r = lax.rsqrt(p[k, k])
            for i in range(k + 1, 8):
                p[i, k] = p[i, k] * r
            for i in range(k + 1, 8):
                for j in range(k + 1, i + 1):
                    p[i, j] = p[i, j] - p[i, k] * p[j, k]
            d[k] = d[k] * r
            e[k] = e[k] * r
            for i in range(k + 1, 8):
                d[i] = d[i] - p[i, k] * d[k]
                e[i] = e[i] - p[i, k] * e[k]
            d_ref[b + k:b + k + 1, :] = d[k][:1]
            e_ref[b + k:b + k + 1, :] = e[k][:1]
            if more:
                t[k] = t[k] * r
                for i in range(k + 1, 8):
                    t[i] = t[i] - p[i, k] * t[k]
                nd = nd - t[k] * d[k]
                ne = ne - t[k] * e[k]
        if more:
            d_ref[b + 8:b + 16, :] = nd
            e_ref[b + 8:b + 16, :] = ne
        if s + 2 < strips:
            lo_row = b + 16
            w = jnp.concatenate([d_ref[b:b + 8, :], e_ref[b:b + 8, :]], axis=1)
            wh = w.astype(BF16).astype(F32)
            wl = w - wh
            rhs = jnp.concatenate([wh, wl, wh, wl], axis=0).astype(BF16)
            uh, ul = wh[:, :NT], wl[:, :NT]
            lhs = jnp.concatenate([uh, uh, ul, ul], axis=0).astype(BF16)
            upd = bdot(lhs, rhs, TN)[lo_row:, :]
            d_ref[lo_row:, :] = d_ref[lo_row:, :] - upd[:, :NT]
            e_ref[lo_row:, :] = e_ref[lo_row:, :] - upd[:, NT:]


def reduce_block(a_ref, z_ref, linv_ref, d_ref, e_ref, p_ref, keep_factor, during):
    size = a_ref.shape[1]
    blocks = size // NT
    rows = a_ref.shape[0]

    def step(j, carry):
        at = pl.ds(pl.multiple_of(j * NT, NT), NT)
        d_ref[...] = a_ref[at, at]
        factor_diag(d_ref, e_ref, p_ref)
        linv_ref[j] = e_ref[...]
        if keep_factor:
            a_ref[at, at] = d_ref[...].T
        for i in range(blocks):

            @pl.when(j == i)
            def _():
                during(i)
                cols = slice(i * NT, (i + 1) * NT)
                below = (i + 1) * NT
                panel = dot3(split(a_ref[below:, cols]), split(e_ref[...]), NTR)
                a_ref[below:, cols] = panel
                ph, pw = split(a_ref[below:, :below] if i == 1 else panel)
                for k in range(i + 1, 2 if i == 0 else blocks):
                    r = k * NT
                    o = r - below
                    new = dot3((ph[o:], pw[o:]), (ph[o:o + NT], pw[o:o + NT]), NTR)
                    a_ref[r:, r:r + NT] = a_ref[r:, r:r + NT] - new

        return carry

    lax.fori_loop(0, blocks, step, 0)
    for i in reversed(range(blocks)):
        cols = slice(i * NT, (i + 1) * NT)
        below = (i + 1) * NT
        acc = a_ref[size:rows, cols]
        if below < size:
            acc = acc - dot3(split(z_ref[:, below:]), split(a_ref[below:size, cols]), NN)
        z_ref[:, cols] = dot3(split(acc), split(linv_ref[i]), NN)


def wrap(axis, by):
    size = lax.axis_size(axis)
    return lax.rem(lax.axis_index(axis) + (by + size), size)


def plus(a, b):
    return (a[0] + b[0], a[1] + b[1])


def times(k, a):
    return (k * a[0], k * a[1])


RINGS = ((0, 1), (1, 0))
WHOLE, TOP, BOTTOM = (0, 2), (0, 1), (1, 2)


def relay_plan():
    messages, rounds = [], []

    def leave(towards, block, rows, part):
        messages.append((towards, block, rows, part))
        return len(messages) - 1

    def relay(axis, block, part):
        return [
            leave(axis, plus(block, times(-1, axis)), TOP, part),
            leave(times(-1, axis), plus(block, axis), BOTTOM, part),
        ]

    def both(axis, block, part):
        return [leave(axis, block, WHOLE, part), leave(times(-1, axis), block, WHOLE, part)]

    own = [m for axis in RINGS for m in both(axis, (0, 0), None)]
    rounds.append(([], own))
    far, sides, starts = [], [], []
    for part in range(2):
        a, b = RINGS[part], RINGS[1 - part]
        far.append(relay(a, (0, 0), part))
        sides.append([both(b, times(-1, a), part), both(b, a, part)])
        starts += far[part] + sides[part][0] + sides[part][1] + relay(b, (0, 0), part)
    rounds.append((own, starts))
    comes, starts, last = [], [], []
    for part in range(2):
        a, b = RINGS[part], RINGS[1 - part]
        comes += far[part] + sides[part][0] + sides[part][1]
        last.append(both(b, times(2, a), part))
        starts += last[part] + relay(b, times(-1, a), part) + relay(b, a, part)
    rounds.append((comes, starts))
    starts = []
    for part in range(2):
        a, b = RINGS[part], RINGS[1 - part]
        starts += relay(b, times(2, a), part)
    rounds.append((last[0] + last[1], starts))
    seen = {m for came, _ in rounds for m in came}
    rounds.append(([m for m in range(len(messages)) if m not in seen], []))
    return messages, rounds


def direct_plan():
    messages, starts = [], []
    hops = [[axis, times(-1, axis), times(2, axis)] for axis in RINGS]
    for ring in hops:
        for hop in ring:
            messages.append((hop, (0, 0), WHOLE, None))
    own = list(range(len(messages)))
    for part in range(2):
        for hop in hops[part]:
            for onward in hops[1 - part]:
                starts.append(len(messages))
                messages.append((onward, times(-1, hop), WHOLE, part))
    return messages, [([], own), (own, starts), (starts, [])]


RELAY, DIRECT = relay_plan(), direct_plan()
START = 1
EARLY_AT = (1, 3)
LATE_AT = (0, 2, 4)
SLOTS = max(len(RELAY[0]), len(DIRECT[0]))


def col_device(by):
    me = lax.axis_index("col")
    y, x = lax.div(me, SIDE), lax.rem(me, SIDE)
    return lax.rem(y + (by[0] + SIDE), SIDE) * SIDE + lax.rem(x + (by[1] + SIDE), SIDE)


def gather_round(plan, k, *arrays):
    messages, rounds = plan

    def message(i, src, full, cols, lowest, send, recv):
        towards, block, rows, part = messages[i]
        height = full.shape[0] // SIDE**2
        begin, length = rows[0] * height // 2, (rows[1] - rows[0]) * height // 2
        at = pl.ds(pl.multiple_of(col_device(block) * height + begin, 8), length)
        half = (cols[1] - cols[0]) // 2
        over = pl.ds(*((cols[0], 2 * half) if part is None else (cols[0] + part * half, half)))
        there = full.at[at, over]
        return pltpu.make_async_remote_copy(
            src_ref=src.at[:, over] if block == (0, 0) and part is None else there,
            dst_ref=there,
            send_sem=send.at[i],
            recv_sem=recv.at[i],
            device_id={"col": col_device(towards)},
            device_id_type=MESH,
        )

    def each(indices, act, seen_from_here):
        for array in arrays:
            for i in indices:
                towards, block = messages[i][:2]
                moved = block if seen_from_here else plus(block, times(-1, towards))
                if array[3] == 0:
                    act(message(i, *array))
                else:
                    pl.when(col_device(moved) >= array[3])(lambda: act(message(i, *array)))

    comes, starts = rounds[k]
    each(comes, lambda copy: copy.wait_recv(), False)
    each(starts, lambda copy: copy.start(), True)
    if k == len(rounds) - 1:
        each(range(len(messages)), lambda copy: copy.wait_send(), True)


def enter(others):
    peers = [{"col": col_device(times(k, axis))} for axis in RINGS for k in (1, -1, 2)] + others
    barrier = pltpu.get_barrier_semaphore()
    for peer in peers:
        pl.semaphore_signal(barrier, inc=1, device_id=peer, device_id_type=MESH)
    pl.semaphore_wait(barrier, len(peers))


def kernel(diag, left, right, blocks, solved, *scratch):
    (a_one, a_two, left_full, right_full, first, second, z_ref, linv_ref, d_ref, e_ref, p_ref) = scratch[:11]
    (lgram, rgram, upper, mirror, reduced, came, grams, send, recv, tsend, trecv) = scratch[11:]
    height, size = left.shape
    near, rest = (0, 2 * NT), (2 * NT, size)
    mine = pl.ds(pl.multiple_of(lax.axis_index("col") * height, 16), height)
    enter([{"tm": wrap("tm", 1)}, {"tm": wrap("tm", -1)}])

    def factor(level, a_ref, pivot_rows, early_rows, early_full, late_rows, late_full, ready):
        full = a_ref.at[pl.ds(0, size)]
        sems = [(send.at[level, i], recv.at[level, i]) for i in range(4)]
        head = (pivot_rows, full, near, 0, *sems[0])
        tail = (pivot_rows, full, rest, 2 * NT // height, *sems[1])
        early = (early_rows, early_full, (0, size), 0, *sems[2])
        late = (late_rows, late_full, (0, size), 0, *sems[3])
        gather_round(DIRECT, 1, head)
        gather_round(DIRECT, 0, tail)
        a_ref[mine, :] = pivot_rows[...]
        ready()
        gather_round(RELAY, 0, late)
        gather_round(DIRECT, 2, head)
        gather_round(DIRECT, 1, tail)
        if START:
            gather_round(RELAY, 1, early)

        def during(j):
            if j == 1:
                gather_round(DIRECT, 2, tail)
            if j in EARLY_AT:
                gather_round(RELAY, START + 1 + EARLY_AT.index(j), early)
            if j in LATE_AT:
                gather_round(RELAY, 1 + LATE_AT.index(j), late)

        reduce_block(a_ref, z_ref, linv_ref, d_ref, e_ref, p_ref, level == 0, during)
        gather_round(RELAY, 4, early, late)

    def begin(level, a_ref, pivot_rows):
        full = a_ref.at[pl.ds(0, size)]
        gather_round(DIRECT, 0, (pivot_rows, full, near, 0, send.at[level, 0], recv.at[level, 0]))

    def begin_early(level, rows, full):
        gather_round(RELAY, 0, (rows, full, (0, size), 0, send.at[level, 2], recv.at[level, 2]))

    def over(i, by, src, dst):
        return pltpu.make_async_remote_copy(
            src_ref=src,
            dst_ref=dst,
            send_sem=tsend.at[i],
            recv_sem=trecv.at[i],
            device_id={"tm": wrap("tm", by)},
            device_id_type=MESH,
        )

    odd = diag.at[1]
    begin(0, a_one, odd)
    begin_early(0, left, left_full)

    def ready_one():
        a_one[size:size + height, :] = left[...]
        a_one[size + height:, :] = right[...]
        left_full[mine, :] = left[...]
        right_full[mine, :] = right[...]

    factor(0, a_one, odd, left, left_full, right, right_full, ready_one)

    z = split(z_ref[...])
    head_gram = over(0, 1, rgram.at[:, pl.ds(0, 2 * NT)], came.at[0, :, pl.ds(0, 2 * NT)])
    tail_gram = over(1, 1, rgram.at[:, pl.ds(2 * NT, size - 2 * NT)], came.at[0, :, pl.ds(2 * NT, size - 2 * NT)])
    over_upper = over(2, 1, upper, first.at[mine])

    def with_right(cols):
        both = dot3(z, split(right_full[cols, :]), NTR)
        upper[:, cols] = -both[:height]
        rgram[:, cols] = both[height:]

    def with_left(cols):
        both = dot3(z, split(left_full[cols, :]), NTR)
        lgram[:, cols] = both[:height]
        mirror[:, cols] = -both[height:]

    parts = [slice(n, n + 2 * NT) for n in range(0, size, 2 * NT)]
    with_right(parts[0])
    head_gram.start()
    for cols in parts[1:]:
        with_right(cols)
    tail_gram.start()
    over_upper.start()
    with_left(parts[0])
    head_gram.wait_recv()
    reduced[:, parts[0]] = diag[0, :, parts[0]] - lgram[:, parts[0]] - came[0, :, parts[0]]
    begin(1, a_two, reduced)
    for cols in parts[1:]:
        with_left(cols)
    begin_early(1, mirror, second)
    tail_gram.wait_recv()
    reduced[:, 2 * NT:] = diag[0, :, 2 * NT:] - lgram[:, 2 * NT:] - came[0, :, 2 * NT:]
    row = lax.axis_index("col") * height + lax.broadcasted_iota(jnp.int32, (height, size), 0)
    col = lax.broadcasted_iota(jnp.int32, (height, size), 1)
    blocks[1] = jnp.where(col <= row, a_one[mine, :], 0.0)
    solved[0] = a_one[size:size + height, :]
    solved[1] = a_one[size + height:, :]

    def ready_two():
        second[mine, :] = mirror[...]
        a_two[size + height:, :] = mirror[...]
        over_upper.wait_recv()
        a_two[size:size + height, :] = first[mine, :]

    factor(1, a_two, reduced, mirror, second, first.at[mine], first, ready_two)

    zs = [split(z_ref[i * height:(i + 1) * height, :]) for i in range(2)]
    back = []
    for n, cols in enumerate(parts):
        there = pl.ds(n * 2 * NT, 2 * NT)
        for i, (full, by) in enumerate(((first, -1), (second, 1))):
            grams[i, :, cols] = dot3(zs[i], split(full[cols, :]), NTR)
            back.append(over(3 + 2 * n + i, by, grams.at[i, :, there], came.at[1 + i, :, there]))
            back[-1].start()
    for copy in (head_gram, tail_gram, over_upper):
        copy.wait_send()
    for copy in back:
        copy.wait()
    blocks[0] = reduced[...] - came[1] - came[2]


def solution(mesh):
    def shards(diag_blocks, left_blocks, right_blocks):
        height, size = left_blocks.shape[1:]
        part, full = (height, size), (size, size)
        tall = (size + 2 * height, size)
        shapes = [tall, tall, full, full, full, full, (2 * height, size), (size // NT, NT, NT)]
        shapes += [(NT, NT)] * 3 + [part] * 5 + [(3, *part), (2, *part)]
        sems = [pltpu.SemaphoreType.DMA((2, 4, SLOTS))] * 2 + [pltpu.SemaphoreType.DMA((16,))] * 2
        blocks, solved = pl.pallas_call(
            kernel,
            out_shape=[jax.ShapeDtypeStruct((2, *part), F32)] * 2,
            in_specs=[pl.BlockSpec(memory_space=pltpu.VMEM)] * 3,
            out_specs=[pl.BlockSpec(memory_space=pltpu.VMEM)] * 2,
            scratch_shapes=[pltpu.VMEM(s, F32) for s in shapes] + sems,
            compiler_params=pltpu.CompilerParams(
                vmem_limit_bytes=56 << 20, collective_id=0, has_side_effects=True
            ),
        )(diag_blocks, left_blocks[0], right_blocks[0])
        return blocks, solved[None]

    in_specs = (P("tm", "col", None), P("tm", "col", None), P("tm", "col", None))
    out_specs = (P("tm", "col", None), P("tm", None, "col", None))
    return jax.shard_map(shards, mesh=mesh, in_specs=in_specs, out_specs=out_specs, check_vma=False)
```

```python
import jax
import jax.numpy as jnp
from jax import lax
from jax.experimental import pallas as pl
from jax.experimental.pallas import tpu as pltpu
from jax.sharding import PartitionSpec as P

F32 = jnp.float32
BF16 = jnp.bfloat16
NT = 128
SIDE = 4
MESH = pl.DeviceIdType.MESH
NN = (((1,), (0,)), ((), ()))
NTR = (((1,), (1,)), ((), ()))
TN = (((0,), (0,)), ((), ()))


def split(x):
    hi = x.astype(BF16)
    lo = (x - hi.astype(F32)).astype(BF16)
    return hi, lo


def bdot(a, b, dims):
    return lax.dot_general(a, b, dims, preferred_element_type=F32)


def dot3(a, b, dims):
    ah, al = a
    bh, bl = b
    return bdot(ah, bh, dims) + (bdot(ah, bl, dims) + bdot(al, bh, dims))


def lane(rows, j):
    return jnp.broadcast_to(rows[:, j:j + 1], (8, NT))

def factor_diag(d_ref, e_ref, p_ref, q_ref):
    row = lax.broadcasted_iota(jnp.int32, (NT, NT), 0)
    col = lax.broadcasted_iota(jnp.int32, (NT, NT), 1)
    e_ref[...] = jnp.where(row == col, 1.0, 0.0).astype(F32)
    strips = NT // 8
    for s in range(strips):
        b = 8 * s
        half = 64 * (s % 2)
        strip = d_ref[b:b + 8, :]
        if s == 0:
            for j in range(8):
                p_ref[half + 8 * j:half + 8 * j + 8, :] = lane(strip, b + j)
        p = {(i, j): p_ref[pl.ds(half + 8 * j + i, 8, stride=0), :] for i in range(8) for j in range(i + 1)}
        d = [d_ref[pl.ds(b + i, 8, stride=0), :] for i in range(8)]
        e = [e_ref[pl.ds(b + i, 8, stride=0), :] for i in range(8)]
        ahead = range(s + 1, min(strips, s + GROUP - s % GROUP + LOOK))
        nd = {q: d_ref[8 * q:8 * q + 8, :] for q in ahead}
        ne = {q: e_ref[8 * q:8 * q + 8, :] for q in ahead}
        t = {q: [lane(nd[q], b + k) for k in range(8)] for q in ahead}
        nxt = s + 1 < strips
        if nxt:
            c = [lane(nd[s + 1], b + 8 + j) for j in range(8)]
        for k in range(8):
            r = lax.rsqrt(p[k, k])
            for i in range(k + 1, 8):
                p[i, k] = p[i, k] * r
            for i in range(k + 1, 8):
                for j in range(k + 1, i + 1):
                    p[i, j] = p[i, j] - p[i, k] * p[j, k]
            d[k] = d[k] * r
            e[k] = e[k] * r
            for i in range(k + 1, 8):
                d[i] = d[i] - p[i, k] * d[k]
                e[i] = e[i] - p[i, k] * e[k]
            d_ref[b + k:b + k + 1, :] = d[k][:1]
            e_ref[b + k:b + k + 1, :] = e[k][:1]
            for q in ahead:
                t[q][k] = t[q][k] * r
                for i in range(k + 1, 8):
                    t[q][i] = t[q][i] - p[i, k] * t[q][k]
                nd[q] = nd[q] - t[q][k] * d[k]
                ne[q] = ne[q] - t[q][k] * e[k]
            if nxt:
                q_ref[half + 8 * k:half + 8 * k + 8, :] = t[s + 1][k]
                for j in range(8):
                    c[j] = c[j] - t[s + 1][k] * q_ref[pl.ds(half + 8 * k + j, 8, stride=0), :]
        if nxt:
            for j in range(8):
                p_ref[64 - half + 8 * j:64 - half + 8 * j + 8, :] = c[j]
        for q in ahead:
            d_ref[8 * q:8 * q + 8, :] = nd[q]
            e_ref[8 * q:8 * q + 8, :] = ne[q]
        far = s + 1 + LOOK
        if s % GROUP == GROUP - 1 and far < strips:
            lo_row = 8 * far
            top = b + 8 - 8 * GROUP
            w = jnp.concatenate([d_ref[top:b + 8, :], e_ref[top:b + 8, :]], axis=1)
            wh = w.astype(BF16).astype(F32)
            wl = w - wh
            rhs = jnp.concatenate([wh, wl, wh, wl], axis=0).astype(BF16)
            uh, ul = wh[:, :NT], wl[:, :NT]
            lhs = jnp.concatenate([uh, uh, ul, ul], axis=0).astype(BF16)
            upd = bdot(lhs, rhs, TN)[lo_row:, :]
            d_ref[lo_row:, :] = d_ref[lo_row:, :] - upd[:, :NT]
            e_ref[lo_row:, :] = e_ref[lo_row:, :] - upd[:, NT:]


def reduce_block(a_ref, z_ref, linv_ref, d_ref, e_ref, p_ref, q_ref, keep_factor, during):
    size = a_ref.shape[1]
    blocks = size // NT
    rows = a_ref.shape[0]

    def step(j, carry):
        at = pl.ds(pl.multiple_of(j * NT, NT), NT)
        d_ref[...] = a_ref[at, at]
        factor_diag(d_ref, e_ref, p_ref, q_ref)
        linv_ref[j] = e_ref[...]
        if keep_factor:
            a_ref[at, at] = d_ref[...].T
        for i in range(blocks):

            @pl.when(j == i)
            def _():
                during(i)
                cols = slice(i * NT, (i + 1) * NT)
                below = (i + 1) * NT
                panel = dot3(split(a_ref[below:, cols]), split(e_ref[...]), NTR)
                a_ref[below:, cols] = panel
                ph, pw = split(a_ref[below:, :below] if i == 1 else panel)
                for k in range(i + 1, 2 if i == 0 else blocks):
                    r = k * NT
                    o = r - below
                    new = dot3((ph[o:], pw[o:]), (ph[o:o + NT], pw[o:o + NT]), NTR)
                    a_ref[r:, r:r + NT] = a_ref[r:, r:r + NT] - new

        return carry

    lax.fori_loop(0, blocks, step, 0)
    for i in reversed(range(blocks)):
        cols = slice(i * NT, (i + 1) * NT)
        below = (i + 1) * NT
        acc = a_ref[size:rows, cols]
        if below < size:
            acc = acc - dot3(split(z_ref[:, below:]), split(a_ref[below:size, cols]), NN)
        z_ref[:, cols] = dot3(split(acc), split(linv_ref[i]), NN)


def wrap(axis, by):
    size = lax.axis_size(axis)
    return lax.rem(lax.axis_index(axis) + (by + size), size)


def plus(a, b):
    return (a[0] + b[0], a[1] + b[1])


def times(k, a):
    return (k * a[0], k * a[1])


RINGS = ((0, 1), (1, 0))
WHOLE, TOP, BOTTOM = (0, 2), (0, 1), (1, 2)


def relay_plan():
    messages, rounds = [], []

    def leave(towards, block, rows, part):
        messages.append((towards, block, rows, part))
        return len(messages) - 1

    def relay(axis, block, part):
        return [
            leave(axis, plus(block, times(-1, axis)), TOP, part),
            leave(times(-1, axis), plus(block, axis), BOTTOM, part),
        ]

    def both(axis, block, part):
        return [leave(axis, block, WHOLE, part), leave(times(-1, axis), block, WHOLE, part)]

    own = [m for axis in RINGS for m in both(axis, (0, 0), None)]
    rounds.append(([], own))
    far, sides, starts = [], [], []
    for part in range(2):
        a, b = RINGS[part], RINGS[1 - part]
        far.append(relay(a, (0, 0), part))
        sides.append([both(b, times(-1, a), part), both(b, a, part)])
        starts += far[part] + sides[part][0] + sides[part][1] + relay(b, (0, 0), part)
    rounds.append((own, starts))
    comes, starts, last = [], [], []
    for part in range(2):
        a, b = RINGS[part], RINGS[1 - part]
        comes += far[part] + sides[part][0] + sides[part][1]
        last.append(both(b, times(2, a), part))
        starts += last[part] + relay(b, times(-1, a), part) + relay(b, a, part)
    rounds.append((comes, starts))
    starts = []
    for part in range(2):
        a, b = RINGS[part], RINGS[1 - part]
        starts += relay(b, times(2, a), part)
    rounds.append((last[0] + last[1], starts))
    seen = {m for came, _ in rounds for m in came}
    rounds.append(([m for m in range(len(messages)) if m not in seen], []))
    return messages, rounds


def direct_plan():
    messages, starts = [], []
    hops = [[axis, times(-1, axis), times(2, axis)] for axis in RINGS]
    for ring in hops:
        for hop in ring:
            messages.append((hop, (0, 0), WHOLE, None))
    own = list(range(len(messages)))
    for part in range(2):
        for hop in hops[part]:
            for onward in hops[1 - part]:
                starts.append(len(messages))
                messages.append((onward, times(-1, hop), WHOLE, part))
    return messages, [([], own), (own, starts), (starts, [])]


RELAY, DIRECT = relay_plan(), direct_plan()
START = 1
EARLY_AT = (2, 4)
LATE_AT = (1, 3, 5)
GROUP, LOOK = 2, 2
SLOTS = max(len(RELAY[0]), len(DIRECT[0]))


def col_device(by):
    me = lax.axis_index("col")
    y, x = lax.div(me, SIDE), lax.rem(me, SIDE)
    return lax.rem(y + (by[0] + SIDE), SIDE) * SIDE + lax.rem(x + (by[1] + SIDE), SIDE)


def gather_round(plan, k, *arrays):
    messages, rounds = plan

    def message(i, src, full, cols, lowest, send, recv):
        towards, block, rows, part = messages[i]
        height = full.shape[0] // SIDE**2
        begin, length = rows[0] * height // 2, (rows[1] - rows[0]) * height // 2
        at = pl.ds(pl.multiple_of(col_device(block) * height + begin, 8), length)
        half = (cols[1] - cols[0]) // 2
        over = pl.ds(*((cols[0], 2 * half) if part is None else (cols[0] + part * half, half)))
        there = full.at[at, over]
        return pltpu.make_async_remote_copy(
            src_ref=src.at[:, over] if block == (0, 0) and part is None else there,
            dst_ref=there,
            send_sem=send.at[i],
            recv_sem=recv.at[i],
            device_id={"col": col_device(towards)},
            device_id_type=MESH,
        )

    def each(indices, act, seen_from_here):
        for array in arrays:
            for i in indices:
                towards, block = messages[i][:2]
                moved = block if seen_from_here else plus(block, times(-1, towards))
                if array[3] == 0:
                    act(message(i, *array))
                else:
                    pl.when(col_device(moved) >= array[3])(lambda: act(message(i, *array)))

    comes, starts = rounds[k]
    each(comes, lambda copy: copy.wait_recv(), False)
    each(starts, lambda copy: copy.start(), True)
    if k == len(rounds) - 1:
        each(range(len(messages)), lambda copy: copy.wait_send(), True)


def enter(others):
    peers = [{"col": col_device(times(k, axis))} for axis in RINGS for k in (1, -1, 2)] + others
    barrier = pltpu.get_barrier_semaphore()
    for peer in peers:
        pl.semaphore_signal(barrier, inc=1, device_id=peer, device_id_type=MESH)
    pl.semaphore_wait(barrier, len(peers))


def kernel(diag, left, right, blocks, solved, *scratch):
    (a_one, a_two, left_full, right_full, first, second, z_ref, linv_ref, d_ref, e_ref, p_ref, q_ref) = scratch[:12]
    (lgram, rgram, upper, mirror, reduced, came, grams, send, recv, tsend, trecv) = scratch[12:]
    height, size = left.shape
    near, rest = (0, 2 * NT), (2 * NT, size)
    mine = pl.ds(pl.multiple_of(lax.axis_index("col") * height, 16), height)
    enter([{"tm": wrap("tm", 1)}, {"tm": wrap("tm", -1)}])

    def factor(level, a_ref, pivot_rows, early_rows, early_full, late_rows, late_full, ready):
        full = a_ref.at[pl.ds(0, size)]
        sems = [(send.at[level, i], recv.at[level, i]) for i in range(4)]
        head = (pivot_rows, full, near, 0, *sems[0])
        tail = (pivot_rows, full, rest, 2 * NT // height, *sems[1])
        early = (early_rows, early_full, (0, size), 0, *sems[2])
        late = (late_rows, late_full, (0, size), 0, *sems[3])
        gather_round(DIRECT, 1, head)
        gather_round(DIRECT, 0, tail)
        a_ref[mine, :] = pivot_rows[...]
        ready()
        gather_round(RELAY, 0, late)
        gather_round(DIRECT, 2, head)
        gather_round(DIRECT, 1, tail)
        if START:
            gather_round(RELAY, 1, early)

        def during(j):
            if j == 1:
                gather_round(DIRECT, 2, tail)
            if j in EARLY_AT:
                gather_round(RELAY, START + 1 + EARLY_AT.index(j), early)
            if j in LATE_AT:
                gather_round(RELAY, 1 + LATE_AT.index(j), late)

        reduce_block(a_ref, z_ref, linv_ref, d_ref, e_ref, p_ref, q_ref, level == 0, during)
        gather_round(RELAY, 4, early, late)

    def begin(level, a_ref, pivot_rows):
        full = a_ref.at[pl.ds(0, size)]
        gather_round(DIRECT, 0, (pivot_rows, full, near, 0, send.at[level, 0], recv.at[level, 0]))

    def begin_early(level, rows, full):
        gather_round(RELAY, 0, (rows, full, (0, size), 0, send.at[level, 2], recv.at[level, 2]))

    def over(i, by, src, dst):
        return pltpu.make_async_remote_copy(
            src_ref=src,
            dst_ref=dst,
            send_sem=tsend.at[i],
            recv_sem=trecv.at[i],
            device_id={"tm": wrap("tm", by)},
            device_id_type=MESH,
        )

    odd = diag.at[1]
    begin(0, a_one, odd)
    begin_early(0, left, left_full)

    def ready_one():
        a_one[size:size + height, :] = left[...]
        a_one[size + height:, :] = right[...]
        left_full[mine, :] = left[...]
        right_full[mine, :] = right[...]

    factor(0, a_one, odd, left, left_full, right, right_full, ready_one)

    z = split(z_ref[...])
    head_gram = over(0, 1, rgram.at[:, pl.ds(0, 2 * NT)], came.at[0, :, pl.ds(0, 2 * NT)])
    tail_gram = over(1, 1, rgram.at[:, pl.ds(2 * NT, size - 2 * NT)], came.at[0, :, pl.ds(2 * NT, size - 2 * NT)])
    over_upper = over(2, 1, upper, first.at[mine])

    def with_right(cols):
        both = dot3(z, split(right_full[cols, :]), NTR)
        upper[:, cols] = -both[:height]
        rgram[:, cols] = both[height:]

    def with_left(cols):
        both = dot3(z, split(left_full[cols, :]), NTR)
        lgram[:, cols] = both[:height]
        mirror[:, cols] = -both[height:]

    parts = [slice(n, n + 2 * NT) for n in range(0, size, 2 * NT)]
    with_right(parts[0])
    head_gram.start()
    for cols in parts[1:]:
        with_right(cols)
    tail_gram.start()
    over_upper.start()
    with_left(parts[0])
    head_gram.wait_recv()
    reduced[:, parts[0]] = diag[0, :, parts[0]] - lgram[:, parts[0]] - came[0, :, parts[0]]
    begin(1, a_two, reduced)
    for cols in parts[1:]:
        with_left(cols)
    begin_early(1, mirror, second)
    tail_gram.wait_recv()
    reduced[:, 2 * NT:] = diag[0, :, 2 * NT:] - lgram[:, 2 * NT:] - came[0, :, 2 * NT:]
    row = lax.axis_index("col") * height + lax.broadcasted_iota(jnp.int32, (height, size), 0)
    col = lax.broadcasted_iota(jnp.int32, (height, size), 1)
    blocks[1] = jnp.where(col <= row, a_one[mine, :], 0.0)
    solved[0] = a_one[size:size + height, :]
    solved[1] = a_one[size + height:, :]

    def ready_two():
        second[mine, :] = mirror[...]
        a_two[size + height:, :] = mirror[...]
        over_upper.wait_recv()
        a_two[size:size + height, :] = first[mine, :]

    factor(1, a_two, reduced, mirror, second, first.at[mine], first, ready_two)

    zs = [split(z_ref[i * height:(i + 1) * height, :]) for i in range(2)]
    back = []
    for n, cols in enumerate(parts):
        there = pl.ds(n * 2 * NT, 2 * NT)
        for i, (full, by) in enumerate(((first, -1), (second, 1))):
            grams[i, :, cols] = dot3(zs[i], split(full[cols, :]), NTR)
            back.append(over(3 + 2 * n + i, by, grams.at[i, :, there], came.at[1 + i, :, there]))
            back[-1].start()
    for copy in (head_gram, tail_gram, over_upper):
        copy.wait_send()
    for copy in back:
        copy.wait()
    blocks[0] = reduced[...] - came[1] - came[2]


def solution(mesh):
    def shards(diag_blocks, left_blocks, right_blocks):
        height, size = left_blocks.shape[1:]
        part, full = (height, size), (size, size)
        tall = (size + 2 * height, size)
        shapes = [tall, tall, full, full, full, full, (2 * height, size), (size // NT, NT, NT)]
        shapes += [(NT, NT)] * 4 + [part] * 5 + [(3, *part), (2, *part)]
        sems = [pltpu.SemaphoreType.DMA((2, 4, SLOTS))] * 2 + [pltpu.SemaphoreType.DMA((16,))] * 2
        blocks, solved = pl.pallas_call(
            kernel,
            out_shape=[jax.ShapeDtypeStruct((2, *part), F32)] * 2,
            in_specs=[pl.BlockSpec(memory_space=pltpu.VMEM)] * 3,
            out_specs=[pl.BlockSpec(memory_space=pltpu.VMEM)] * 2,
            scratch_shapes=[pltpu.VMEM(s, F32) for s in shapes] + sems,
            compiler_params=pltpu.CompilerParams(
                vmem_limit_bytes=56 << 20, collective_id=0, has_side_effects=True
            ),
        )(diag_blocks, left_blocks[0], right_blocks[0])
        return blocks, solved[None]

    in_specs = (P("tm", "col", None), P("tm", "col", None), P("tm", "col", None))
    out_specs = (P("tm", "col", None), P("tm", None, "col", None))
    return jax.shard_map(shards, mesh=mesh, in_specs=in_specs, out_specs=out_specs, check_vma=False)
```

```python
import jax
import jax.numpy as jnp
from jax import lax
from jax.experimental import pallas as pl
from jax.experimental.pallas import tpu as pltpu
from jax.sharding import PartitionSpec as P

F32 = jnp.float32
BF16 = jnp.bfloat16
NT = 128
SIDE = 4
MESH = pl.DeviceIdType.MESH
NN = (((1,), (0,)), ((), ()))
NTR = (((1,), (1,)), ((), ()))
TN = (((0,), (0,)), ((), ()))


def split(x):
    hi = x.astype(BF16)
    lo = (x - hi.astype(F32)).astype(BF16)
    return hi, lo


def bdot(a, b, dims):
    return lax.dot_general(a, b, dims, preferred_element_type=F32)


def dot3(a, b, dims):
    ah, al = a
    bh, bl = b
    return bdot(ah, bh, dims) + (bdot(ah, bl, dims) + bdot(al, bh, dims))


def lane(rows, j):
    return jnp.broadcast_to(rows[:, j:j + 1], (8, NT))

def factor_diag(d_ref, e_ref, p_ref, q_ref):
    row = lax.broadcasted_iota(jnp.int32, (NT, NT), 0)
    col = lax.broadcasted_iota(jnp.int32, (NT, NT), 1)
    e_ref[...] = jnp.where(row == col, 1.0, 0.0).astype(F32)
    strips = NT // 8
    for s in range(strips):
        b = 8 * s
        half = 64 * (s % 2)
        strip = d_ref[b:b + 8, :]
        if s == 0:
            for j in range(8):
                p_ref[half + 8 * j:half + 8 * j + 8, :] = lane(strip, b + j)
        p = {(i, j): p_ref[pl.ds(half + 8 * j + i, 8, stride=0), :] for i in range(8) for j in range(i + 1)}
        d = [d_ref[pl.ds(b + i, 8, stride=0), :] for i in range(8)]
        e = [e_ref[pl.ds(b + i, 8, stride=0), :] for i in range(8)]
        ahead = range(s + 1, min(strips, s + GROUP - s % GROUP + LOOK))
        nd = {q: d_ref[8 * q:8 * q + 8, :] for q in ahead}
        ne = {q: e_ref[8 * q:8 * q + 8, :] for q in ahead}
        t = {q: [lane(nd[q], b + k) for k in range(8)] for q in ahead}
        nxt = s + 1 < strips
        if nxt:
            c = [lane(nd[s + 1], b + 8 + j) for j in range(8)]
        for k in range(8):
            r = lax.rsqrt(p[k, k])
            for i in range(k + 1, 8):
                p[i, k] = p[i, k] * r
            for i in range(k + 1, 8):
                for j in range(k + 1, i + 1):
                    p[i, j] = p[i, j] - p[i, k] * p[j, k]
            d[k] = d[k] * r
            e[k] = e[k] * r
            for i in range(k + 1, 8):
                d[i] = d[i] - p[i, k] * d[k]
                e[i] = e[i] - p[i, k] * e[k]
            d_ref[b + k:b + k + 1, :] = d[k][:1]
            e_ref[b + k:b + k + 1, :] = e[k][:1]
            for q in ahead:
                t[q][k] = t[q][k] * r
                for i in range(k + 1, 8):
                    t[q][i] = t[q][i] - p[i, k] * t[q][k]
                nd[q] = nd[q] - t[q][k] * d[k]
                ne[q] = ne[q] - t[q][k] * e[k]
            if nxt:
                q_ref[half + 8 * k:half + 8 * k + 8, :] = t[s + 1][k]
                for j in range(8):
                    c[j] = c[j] - t[s + 1][k] * q_ref[pl.ds(half + 8 * k + j, 8, stride=0), :]
        if nxt:
            for j in range(8):
                p_ref[64 - half + 8 * j:64 - half + 8 * j + 8, :] = c[j]
        for q in ahead:
            d_ref[8 * q:8 * q + 8, :] = nd[q]
            e_ref[8 * q:8 * q + 8, :] = ne[q]
        far = s + 1 + LOOK
        if s % GROUP == GROUP - 1 and far < strips:
            lo_row = 8 * far
            top = b + 8 - 8 * GROUP
            w = jnp.concatenate([d_ref[top:b + 8, :], e_ref[top:b + 8, :]], axis=1)
            wh = w.astype(BF16).astype(F32)
            wl = w - wh
            rhs = jnp.concatenate([wh, wl, wh, wl], axis=0).astype(BF16)
            uh, ul = wh[:, :NT], wl[:, :NT]
            lhs = jnp.concatenate([uh, uh, ul, ul], axis=0).astype(BF16)
            upd = bdot(lhs, rhs, TN)[lo_row:, :]
            d_ref[lo_row:, :] = d_ref[lo_row:, :] - upd[:, :NT]
            e_ref[lo_row:, :] = e_ref[lo_row:, :] - upd[:, NT:]


def reduce_block(a_ref, z_ref, linv_ref, d_ref, e_ref, p_ref, q_ref, keep_factor, during):
    size = a_ref.shape[1]
    blocks = size // NT
    rows = a_ref.shape[0]

    def step(j, carry):
        at = pl.ds(pl.multiple_of(j * NT, NT), NT)
        d_ref[...] = a_ref[at, at]
        factor_diag(d_ref, e_ref, p_ref, q_ref)
        linv_ref[j] = e_ref[...]
        if keep_factor:
            a_ref[at, at] = d_ref[...].T
        for i in range(blocks):

            @pl.when(j == i)
            def _():
                during(i)
                cols = slice(i * NT, (i + 1) * NT)
                below = (i + 1) * NT
                panel = dot3(split(a_ref[below:, cols]), split(e_ref[...]), NTR)
                a_ref[below:, cols] = panel
                ph, pw = split(a_ref[below:, :below] if i == 1 else panel)
                for k in range(i + 1, 2 if i == 0 else blocks):
                    r = k * NT
                    o = r - below
                    new = dot3((ph[o:], pw[o:]), (ph[o:o + NT], pw[o:o + NT]), NTR)
                    a_ref[r:, r:r + NT] = a_ref[r:, r:r + NT] - new

        return carry

    lax.fori_loop(0, blocks, step, 0)
    for i in reversed(range(blocks)):
        cols = slice(i * NT, (i + 1) * NT)
        below = (i + 1) * NT
        acc = a_ref[size:rows, cols]
        if below < size:
            acc = acc - dot3(split(z_ref[:, below:]), split(a_ref[below:size, cols]), NN)
        z_ref[:, cols] = dot3(split(acc), split(linv_ref[i]), NN)


def wrap(axis, by):
    size = lax.axis_size(axis)
    return lax.rem(lax.axis_index(axis) + (by + size), size)


def plus(a, b):
    return (a[0] + b[0], a[1] + b[1])


def times(k, a):
    return (k * a[0], k * a[1])


RINGS = ((0, 1), (1, 0))
WHOLE, TOP, BOTTOM = (0, 2), (0, 1), (1, 2)


def relay_plan():
    messages, rounds = [], []

    def leave(towards, block, rows, part):
        messages.append((towards, block, rows, part))
        return len(messages) - 1

    def relay(axis, block, part):
        return [
            leave(axis, plus(block, times(-1, axis)), TOP, part),
            leave(times(-1, axis), plus(block, axis), BOTTOM, part),
        ]

    def both(axis, block, part):
        return [leave(axis, block, WHOLE, part), leave(times(-1, axis), block, WHOLE, part)]

    own = [m for axis in RINGS for m in both(axis, (0, 0), None)]
    own += [leave(times(2, RINGS[part]), (0, 0), WHOLE, part) for part in range(2)]
    rounds.append(([], own))
    sides, starts, relays = [], [], []
    for part in range(2):
        a, b = RINGS[part], RINGS[1 - part]
        for hop in (a, times(-1, a), times(2, a)):
            sides += both(b, hop, part)
        starts += relay(b, (0, 0), part)
    rounds.append((own, sides + starts))
    for part in range(2):
        a, b = RINGS[part], RINGS[1 - part]
        for hop in (a, times(-1, a), times(2, a)):
            relays += relay(b, hop, part)
    rounds.append((sides, relays))
    seen = {m for came, _ in rounds for m in came}
    rounds.append(([m for m in range(len(messages)) if m not in seen], []))
    return messages, rounds


def direct_plan():
    messages, starts = [], []
    hops = [[axis, times(-1, axis), times(2, axis)] for axis in RINGS]
    for ring in hops:
        for hop in ring:
            messages.append((hop, (0, 0), WHOLE, None))
    own = list(range(len(messages)))
    for part in range(2):
        for hop in hops[part]:
            for onward in hops[1 - part]:
                starts.append(len(messages))
                messages.append((onward, times(-1, hop), WHOLE, part))
    return messages, [([], own), (own, starts), (starts, [])]


RELAY, DIRECT = relay_plan(), direct_plan()
START = 1
EARLY_AT = (4,)
LATE_AT = (3, 5)
GROUP, LOOK = 2, 2
SLOTS = max(len(RELAY[0]), len(DIRECT[0]))


def col_device(by):
    me = lax.axis_index("col")
    y, x = lax.div(me, SIDE), lax.rem(me, SIDE)
    return lax.rem(y + (by[0] + SIDE), SIDE) * SIDE + lax.rem(x + (by[1] + SIDE), SIDE)


def gather_round(plan, k, *arrays):
    messages, rounds = plan

    def message(i, src, full, cols, lowest, send, recv):
        towards, block, rows, part = messages[i]
        height = full.shape[0] // SIDE**2
        begin, length = rows[0] * height // 2, (rows[1] - rows[0]) * height // 2
        at = pl.ds(pl.multiple_of(col_device(block) * height + begin, 8), length)
        half = (cols[1] - cols[0]) // 2
        over = pl.ds(*((cols[0], 2 * half) if part is None else (cols[0] + part * half, half)))
        there = full.at[at, over]
        return pltpu.make_async_remote_copy(
            src_ref=src.at[:, over] if block == (0, 0) and k == 0 else there,
            dst_ref=there,
            send_sem=send.at[i],
            recv_sem=recv.at[i],
            device_id={"col": col_device(towards)},
            device_id_type=MESH,
        )

    def each(indices, act, seen_from_here):
        for array in arrays:
            for i in indices:
                towards, block = messages[i][:2]
                moved = block if seen_from_here else plus(block, times(-1, towards))
                if array[3] == 0:
                    act(message(i, *array))
                else:
                    pl.when(col_device(moved) >= array[3])(lambda: act(message(i, *array)))

    comes, starts = rounds[k]
    each(comes, lambda copy: copy.wait_recv(), False)
    each(starts, lambda copy: copy.start(), True)
    if k == len(rounds) - 1:
        each(range(len(messages)), lambda copy: copy.wait_send(), True)


def enter(others):
    peers = [{"col": col_device(times(k, axis))} for axis in RINGS for k in (1, -1, 2)] + others
    barrier = pltpu.get_barrier_semaphore()
    for peer in peers:
        pl.semaphore_signal(barrier, inc=1, device_id=peer, device_id_type=MESH)
    pl.semaphore_wait(barrier, len(peers))


def kernel(diag, left, right, blocks, solved, *scratch):
    (a_one, a_two, left_full, right_full, first, second, z_ref, linv_ref, d_ref, e_ref, p_ref, q_ref) = scratch[:12]
    (lgram, rgram, upper, mirror, reduced, came, grams, send, recv, tsend, trecv) = scratch[12:]
    height, size = left.shape
    near, rest = (0, 2 * NT), (2 * NT, size)
    mine = pl.ds(pl.multiple_of(lax.axis_index("col") * height, 16), height)
    enter([{"tm": wrap("tm", 1)}, {"tm": wrap("tm", -1)}])

    def factor(level, a_ref, pivot_rows, early_rows, early_full, late_rows, late_full, ready):
        full = a_ref.at[pl.ds(0, size)]
        sems = [(send.at[level, i], recv.at[level, i]) for i in range(4)]
        head = (pivot_rows, full, near, 0, *sems[0])
        tail = (pivot_rows, full, rest, 2 * NT // height, *sems[1])
        early = (early_rows, early_full, (0, size), 0, *sems[2])
        late = (late_rows, late_full, (0, size), 0, *sems[3])
        gather_round(DIRECT, 1, head)
        gather_round(DIRECT, 0, tail)
        a_ref[mine, :] = pivot_rows[...]
        ready()
        gather_round(DIRECT, 2, head)
        gather_round(DIRECT, 1, tail)
        gather_round(RELAY, 0, late)
        if START:
            gather_round(RELAY, 1, early)

        def during(j):
            if j == 1:
                gather_round(DIRECT, 2, tail)
            if j in EARLY_AT:
                gather_round(RELAY, START + 1 + EARLY_AT.index(j), early)
            if j in LATE_AT:
                gather_round(RELAY, 1 + LATE_AT.index(j), late)

        reduce_block(a_ref, z_ref, linv_ref, d_ref, e_ref, p_ref, q_ref, level == 0, during)
        gather_round(RELAY, 3, early)
        return late

    def begin(level, a_ref, pivot_rows):
        full = a_ref.at[pl.ds(0, size)]
        gather_round(DIRECT, 0, (pivot_rows, full, near, 0, send.at[level, 0], recv.at[level, 0]))

    def begin_early(level, rows, full):
        gather_round(RELAY, 0, (rows, full, (0, size), 0, send.at[level, 2], recv.at[level, 2]))

    def over(i, by, src, dst):
        return pltpu.make_async_remote_copy(
            src_ref=src,
            dst_ref=dst,
            send_sem=tsend.at[i],
            recv_sem=trecv.at[i],
            device_id={"tm": wrap("tm", by)},
            device_id_type=MESH,
        )

    odd = diag.at[1]
    begin(0, a_one, odd)
    begin_early(0, right, right_full)

    def ready_one():
        a_one[size:size + height, :] = left[...]
        a_one[size + height:, :] = right[...]
        left_full[mine, :] = left[...]
        right_full[mine, :] = right[...]

    late = factor(0, a_one, odd, right, right_full, left, left_full, ready_one)

    z = split(z_ref[...])
    head_gram = over(0, 1, rgram.at[:, pl.ds(0, 2 * NT)], came.at[0, :, pl.ds(0, 2 * NT)])
    tail_gram = over(1, 1, rgram.at[:, pl.ds(2 * NT, size - 2 * NT)], came.at[0, :, pl.ds(2 * NT, size - 2 * NT)])
    over_upper = over(2, 1, upper, first.at[mine])

    def with_right(cols):
        both = dot3(z, split(right_full[cols, :]), NTR)
        upper[:, cols] = -both[:height]
        rgram[:, cols] = both[height:]

    def with_left(cols):
        both = dot3(z, split(left_full[cols, :]), NTR)
        lgram[:, cols] = both[:height]
        mirror[:, cols] = -both[height:]

    parts = [slice(n, n + 2 * NT) for n in range(0, size, 2 * NT)]
    with_right(parts[0])
    head_gram.start()
    for cols in parts[1:]:
        with_right(cols)
    tail_gram.start()
    over_upper.start()
    gather_round(RELAY, 3, late)
    with_left(parts[0])
    head_gram.wait_recv()
    reduced[:, parts[0]] = diag[0, :, parts[0]] - lgram[:, parts[0]] - came[0, :, parts[0]]
    begin(1, a_two, reduced)
    for cols in parts[1:]:
        with_left(cols)
    begin_early(1, mirror, second)
    tail_gram.wait_recv()
    reduced[:, 2 * NT:] = diag[0, :, 2 * NT:] - lgram[:, 2 * NT:] - came[0, :, 2 * NT:]
    row = lax.axis_index("col") * height + lax.broadcasted_iota(jnp.int32, (height, size), 0)
    col = lax.broadcasted_iota(jnp.int32, (height, size), 1)
    blocks[1] = jnp.where(col <= row, a_one[mine, :], 0.0)
    solved[0] = a_one[size:size + height, :]
    solved[1] = a_one[size + height:, :]

    def ready_two():
        second[mine, :] = mirror[...]
        a_two[size + height:, :] = mirror[...]
        over_upper.wait_recv()
        a_two[size:size + height, :] = first[mine, :]

    late = factor(1, a_two, reduced, mirror, second, first.at[mine], first, ready_two)

    zs = [split(z_ref[i * height:(i + 1) * height, :]) for i in range(2)]
    back = []
    for i, (full, by) in ((1, (second, 1)), (0, (first, -1))):
        if i == 0:
            gather_round(RELAY, 3, late)
        for n, cols in enumerate(parts):
            there = pl.ds(n * 2 * NT, 2 * NT)
            grams[i, :, cols] = dot3(zs[i], split(full[cols, :]), NTR)
            back.append(over(3 + 2 * n + i, by, grams.at[i, :, there], came.at[1 + i, :, there]))
            back[-1].start()
    for copy in (head_gram, tail_gram, over_upper):
        copy.wait_send()
    for copy in back:
        copy.wait()
    blocks[0] = reduced[...] - came[1] - came[2]


def solution(mesh):
    def shards(diag_blocks, left_blocks, right_blocks):
        height, size = left_blocks.shape[1:]
        part, full = (height, size), (size, size)
        tall = (size + 2 * height, size)
        shapes = [tall, tall, full, full, full, full, (2 * height, size), (size // NT, NT, NT)]
        shapes += [(NT, NT)] * 4 + [part] * 5 + [(3, *part), (2, *part)]
        sems = [pltpu.SemaphoreType.DMA((2, 4, SLOTS))] * 2 + [pltpu.SemaphoreType.DMA((16,))] * 2
        blocks, solved = pl.pallas_call(
            kernel,
            out_shape=[jax.ShapeDtypeStruct((2, *part), F32)] * 2,
            in_specs=[pl.BlockSpec(memory_space=pltpu.VMEM)] * 3,
            out_specs=[pl.BlockSpec(memory_space=pltpu.VMEM)] * 2,
            scratch_shapes=[pltpu.VMEM(s, F32) for s in shapes] + sems,
            compiler_params=pltpu.CompilerParams(
                vmem_limit_bytes=56 << 20, collective_id=0, has_side_effects=True
            ),
        )(diag_blocks, left_blocks[0], right_blocks[0])
        return blocks, solved[None]

    in_specs = (P("tm", "col", None), P("tm", "col", None), P("tm", "col", None))
    out_specs = (P("tm", "col", None), P("tm", None, "col", None))
    return jax.shard_map(shards, mesh=mesh, in_specs=in_specs, out_specs=out_specs, check_vma=False)
```

```python
import jax
import jax.numpy as jnp
from jax import lax
from jax.experimental import pallas as pl
from jax.experimental.pallas import tpu as pltpu
from jax.sharding import PartitionSpec as P

F32 = jnp.float32
BF16 = jnp.bfloat16
NT = 128
SIDE = 4
MESH = pl.DeviceIdType.MESH
NN = (((1,), (0,)), ((), ()))
NTR = (((1,), (1,)), ((), ()))
TN = (((0,), (0,)), ((), ()))


def split(x):
    hi = x.astype(BF16)
    lo = (x - hi.astype(F32)).astype(BF16)
    return hi, lo


def bdot(a, b, dims):
    return lax.dot_general(a, b, dims, preferred_element_type=F32)


def dot3(a, b, dims):
    ah, al = a
    bh, bl = b
    return bdot(ah, bh, dims) + (bdot(ah, bl, dims) + bdot(al, bh, dims))


def lane(rows, j):
    return jnp.broadcast_to(rows[:, j:j + 1], (8, NT))

def factor_diag(d_ref, e_ref, p_ref, q_ref):
    row = lax.broadcasted_iota(jnp.int32, (NT, NT), 0)
    col = lax.broadcasted_iota(jnp.int32, (NT, NT), 1)
    e_ref[...] = jnp.where(row == col, 1.0, 0.0).astype(F32)
    strips = NT // 8
    for s in range(strips):
        b = 8 * s
        half = 64 * (s % 2)
        strip = d_ref[b:b + 8, :]
        if s == 0:
            for j in range(8):
                p_ref[half + 8 * j:half + 8 * j + 8, :] = lane(strip, b + j)
        p = {(i, j): p_ref[pl.ds(half + 8 * j + i, 8, stride=0), :] for i in range(8) for j in range(i + 1)}
        d = [d_ref[pl.ds(b + i, 8, stride=0), :] for i in range(8)]
        e = [e_ref[pl.ds(b + i, 8, stride=0), :] for i in range(8)]
        ahead = range(s + 1, min(strips, s + GROUP - s % GROUP + LOOK))
        nd = {q: d_ref[8 * q:8 * q + 8, :] for q in ahead}
        ne = {q: e_ref[8 * q:8 * q + 8, :] for q in ahead}
        t = {q: [lane(nd[q], b + k) for k in range(8)] for q in ahead}
        nxt = s + 1 < strips
        if nxt:
            c = [lane(nd[s + 1], b + 8 + j) for j in range(8)]
        for k in range(8):
            r = lax.rsqrt(p[k, k])
            for i in range(k + 1, 8):
                p[i, k] = p[i, k] * r
            for i in range(k + 1, 8):
                for j in range(k + 1, i + 1):
                    p[i, j] = p[i, j] - p[i, k] * p[j, k]
            d[k] = d[k] * r
            e[k] = e[k] * r
            for i in range(k + 1, 8):
                d[i] = d[i] - p[i, k] * d[k]
                e[i] = e[i] - p[i, k] * e[k]
            d_ref[b + k:b + k + 1, :] = d[k][:1]
            e_ref[b + k:b + k + 1, :] = e[k][:1]
            for q in ahead:
                t[q][k] = t[q][k] * r
                for i in range(k + 1, 8):
                    t[q][i] = t[q][i] - p[i, k] * t[q][k]
                nd[q] = nd[q] - t[q][k] * d[k]
                ne[q] = ne[q] - t[q][k] * e[k]
            if nxt:
                q_ref[half + 8 * k:half + 8 * k + 8, :] = t[s + 1][k]
                for j in range(8):
                    c[j] = c[j] - t[s + 1][k] * q_ref[pl.ds(half + 8 * k + j, 8, stride=0), :]
        if nxt:
            for j in range(8):
                p_ref[64 - half + 8 * j:64 - half + 8 * j + 8, :] = c[j]
        for q in ahead:
            d_ref[8 * q:8 * q + 8, :] = nd[q]
            e_ref[8 * q:8 * q + 8, :] = ne[q]
        far = s + 1 + LOOK
        if s % GROUP == GROUP - 1 and far < strips:
            lo_row = 8 * far
            top = b + 8 - 8 * GROUP
            w = jnp.concatenate([d_ref[top:b + 8, :], e_ref[top:b + 8, :]], axis=1)
            wh = w.astype(BF16).astype(F32)
            wl = w - wh
            rhs = jnp.concatenate([wh, wl, wh, wl], axis=0).astype(BF16)
            uh, ul = wh[:, :NT], wl[:, :NT]
            lhs = jnp.concatenate([uh, uh, ul, ul], axis=0).astype(BF16)
            upd = bdot(lhs, rhs, TN)[lo_row:, :]
            d_ref[lo_row:, :] = d_ref[lo_row:, :] - upd[:, :NT]
            e_ref[lo_row:, :] = e_ref[lo_row:, :] - upd[:, NT:]


def reduce_block(a_ref, z_ref, linv_ref, d_ref, e_ref, p_ref, q_ref, keep_factor, during):
    size = a_ref.shape[1]
    blocks = size // NT
    rows = a_ref.shape[0]

    def step(j, carry):
        at = pl.ds(pl.multiple_of(j * NT, NT), NT)
        d_ref[...] = a_ref[at, at]
        factor_diag(d_ref, e_ref, p_ref, q_ref)
        linv_ref[j] = e_ref[...]
        if keep_factor:
            a_ref[at, at] = d_ref[...].T
        for i in range(blocks):

            @pl.when(j == i)
            def _():
                during(i)
                cols = slice(i * NT, (i + 1) * NT)
                below = (i + 1) * NT
                panel = dot3(split(a_ref[below:, cols]), split(e_ref[...]), NTR)
                a_ref[below:, cols] = panel
                ph, pw = split(a_ref[below:, :below] if i == 1 else panel)
                for k in range(i + 1, 2 if i == 0 else blocks):
                    r = k * NT
                    o = r - below
                    new = dot3((ph[o:], pw[o:]), (ph[o:o + NT], pw[o:o + NT]), NTR)
                    a_ref[r:, r:r + NT] = a_ref[r:, r:r + NT] - new

        return carry

    lax.fori_loop(0, blocks, step, 0)
    for i in reversed(range(blocks)):
        cols = slice(i * NT, (i + 1) * NT)
        below = (i + 1) * NT
        acc = a_ref[size:rows, cols]
        if below < size:
            acc = acc - dot3(split(z_ref[:, below:]), split(a_ref[below:size, cols]), NN)
        z_ref[:, cols] = dot3(split(acc), split(linv_ref[i]), NN)


def wrap(axis, by):
    size = lax.axis_size(axis)
    return lax.rem(lax.axis_index(axis) + (by + size), size)


def plus(a, b):
    return (a[0] + b[0], a[1] + b[1])


def times(k, a):
    return (k * a[0], k * a[1])


RINGS = ((0, 1), (1, 0))
WHOLE, TOP, BOTTOM = (0, 2), (0, 1), (1, 2)


def relay_plan():
    messages, rounds = [], []

    def leave(towards, block, rows, part):
        messages.append((towards, block, rows, part))
        return len(messages) - 1

    def relay(axis, block, part):
        return [
            leave(axis, plus(block, times(-1, axis)), TOP, part),
            leave(times(-1, axis), plus(block, axis), BOTTOM, part),
        ]

    def both(axis, block, part):
        return [leave(axis, block, WHOLE, part), leave(times(-1, axis), block, WHOLE, part)]

    own = [m for axis in RINGS for m in both(axis, (0, 0), None)]
    own += [leave(times(2, RINGS[part]), (0, 0), WHOLE, part) for part in range(2)]
    rounds.append(([], own))
    sides, starts, relays = [], [], []
    for part in range(2):
        a, b = RINGS[part], RINGS[1 - part]
        for hop in (a, times(-1, a), times(2, a)):
            sides += both(b, hop, part)
        starts += relay(b, (0, 0), part)
    rounds.append((own, sides + starts))
    for part in range(2):
        a, b = RINGS[part], RINGS[1 - part]
        for hop in (a, times(-1, a), times(2, a)):
            relays += relay(b, hop, part)
    rounds.append((sides, relays))
    seen = {m for came, _ in rounds for m in came}
    rounds.append(([m for m in range(len(messages)) if m not in seen], []))
    return messages, rounds


def direct_plan():
    messages, starts = [], []
    hops = [[axis, times(-1, axis), times(2, axis)] for axis in RINGS]
    for ring in hops:
        for hop in ring:
            messages.append((hop, (0, 0), WHOLE, None))
    own = list(range(len(messages)))
    for part in range(2):
        for hop in hops[part]:
            for onward in hops[1 - part]:
                starts.append(len(messages))
                messages.append((onward, times(-1, hop), WHOLE, part))
    return messages, [([], own), (own, starts), (starts, [])]


RELAY, DIRECT = relay_plan(), direct_plan()
START = 1
EARLY_AT = (4,)
LATE_AT = (3, 5)
GROUP, LOOK = 2, 2
SLOTS = max(len(RELAY[0]), len(DIRECT[0]))


def col_device(by):
    me = lax.axis_index("col")
    y, x = lax.div(me, SIDE), lax.rem(me, SIDE)
    return lax.rem(y + (by[0] + SIDE), SIDE) * SIDE + lax.rem(x + (by[1] + SIDE), SIDE)


def gather_round(plan, k, *arrays):
    messages, rounds = plan

    def message(i, src, full, cols, lowest, send, recv):
        towards, block, rows, part = messages[i]
        height = full.shape[0] // SIDE**2
        begin, length = rows[0] * height // 2, (rows[1] - rows[0]) * height // 2
        at = pl.ds(pl.multiple_of(col_device(block) * height + begin, 8), length)
        half = (cols[1] - cols[0]) // 2
        over = pl.ds(*((cols[0], 2 * half) if part is None else (cols[0] + part * half, half)))
        there = full.at[at, over]
        return pltpu.make_async_remote_copy(
            src_ref=src.at[:, over] if block == (0, 0) and k == 0 else there,
            dst_ref=there,
            send_sem=send.at[i],
            recv_sem=recv.at[i],
            device_id={"col": col_device(towards)},
            device_id_type=MESH,
        )

    def each(indices, act, seen_from_here):
        for array in arrays:
            for i in indices:
                towards, block = messages[i][:2]
                moved = block if seen_from_here else plus(block, times(-1, towards))
                if array[3] == 0:
                    act(message(i, *array))
                else:
                    pl.when(col_device(moved) >= array[3])(lambda: act(message(i, *array)))

    comes, starts = rounds[k]
    each(comes, lambda copy: copy.wait_recv(), False)
    each(starts, lambda copy: copy.start(), True)
    if k == len(rounds) - 1:
        each(range(len(messages)), lambda copy: copy.wait_send(), True)


def enter(others):
    peers = [{"col": col_device(times(k, axis))} for axis in RINGS for k in (1, -1, 2)] + others
    barrier = pltpu.get_barrier_semaphore()
    for peer in peers:
        pl.semaphore_signal(barrier, inc=1, device_id=peer, device_id_type=MESH)
    pl.semaphore_wait(barrier, len(peers))


def kernel(diag, left, right, blocks, solved, *scratch):
    (a_one, a_two, left_full, right_full, first, second, z_ref, linv_ref, d_ref, e_ref, p_ref, q_ref) = scratch[:12]
    (lgram, rgram, upper, mirror, reduced, came, grams, send, recv, tsend, trecv) = scratch[12:]
    height, size = left.shape
    near = (0, 2 * NT)
    mine = pl.ds(pl.multiple_of(lax.axis_index("col") * height, 16), height)
    enter([{"tm": wrap("tm", 1)}, {"tm": wrap("tm", -1)}])

    def factor(level, a_ref, pivot_rows, early_rows, early_full, late_rows, late_full, ready):
        full = a_ref.at[pl.ds(0, size)]
        sems = [(send.at[level, i], recv.at[level, i]) for i in range(5)]
        head = (pivot_rows, full, near, 0, *sems[0])
        tail = [(pivot_rows, full, (c, c + 2 * NT), c // height, *sems[i]) for c, i in ((2 * NT, 1), (4 * NT, 4))]
        early = (early_rows, early_full, (0, size), 0, *sems[2])
        late = (late_rows, late_full, (0, size), 0, *sems[3])
        gather_round(DIRECT, 1, head)
        gather_round(DIRECT, 0, *tail)
        a_ref[mine, :] = pivot_rows[...]
        ready()
        gather_round(DIRECT, 2, head)
        gather_round(DIRECT, 1, *tail)
        gather_round(RELAY, 0, late)
        if START:
            gather_round(RELAY, 1, early)

        def during(j):
            if j == 1:
                gather_round(DIRECT, 2, *tail)
            if j in EARLY_AT:
                gather_round(RELAY, START + 1 + EARLY_AT.index(j), early)
            if j in LATE_AT:
                gather_round(RELAY, 1 + LATE_AT.index(j), late)

        reduce_block(a_ref, z_ref, linv_ref, d_ref, e_ref, p_ref, q_ref, level == 0, during)
        gather_round(RELAY, 3, early)
        return late

    def begin(level, a_ref, pivot_rows):
        full = a_ref.at[pl.ds(0, size)]
        gather_round(DIRECT, 0, (pivot_rows, full, near, 0, send.at[level, 0], recv.at[level, 0]))

    def begin_early(level, rows, full):
        gather_round(RELAY, 0, (rows, full, (0, size), 0, send.at[level, 2], recv.at[level, 2]))

    def over(i, by, src, dst):
        return pltpu.make_async_remote_copy(
            src_ref=src,
            dst_ref=dst,
            send_sem=tsend.at[i],
            recv_sem=trecv.at[i],
            device_id={"tm": wrap("tm", by)},
            device_id_type=MESH,
        )

    odd = diag.at[1]
    begin(0, a_one, odd)
    begin_early(0, right, right_full)

    def ready_one():
        a_one[size:size + height, :] = left[...]
        a_one[size + height:, :] = right[...]
        left_full[mine, :] = left[...]
        right_full[mine, :] = right[...]

    late = factor(0, a_one, odd, right, right_full, left, left_full, ready_one)

    z = split(z_ref[...])
    head_gram = over(0, 1, rgram.at[:, pl.ds(0, 2 * NT)], came.at[0, :, pl.ds(0, 2 * NT)])
    tail_gram = over(1, 1, rgram.at[:, pl.ds(2 * NT, size - 2 * NT)], came.at[0, :, pl.ds(2 * NT, size - 2 * NT)])
    over_upper = over(2, 1, upper, first.at[mine])

    def with_right(cols):
        both = dot3(z, split(right_full[cols, :]), NTR)
        upper[:, cols] = -both[:height]
        rgram[:, cols] = both[height:]

    def with_left(cols):
        both = dot3(z, split(left_full[cols, :]), NTR)
        lgram[:, cols] = both[:height]
        mirror[:, cols] = -both[height:]

    parts = [slice(n, n + 2 * NT) for n in range(0, size, 2 * NT)]
    with_right(parts[0])
    head_gram.start()
    for cols in parts[1:]:
        with_right(cols)
    tail_gram.start()
    over_upper.start()
    gather_round(RELAY, 3, late)
    with_left(parts[0])
    head_gram.wait_recv()
    reduced[:, parts[0]] = diag[0, :, parts[0]] - lgram[:, parts[0]] - came[0, :, parts[0]]
    begin(1, a_two, reduced)
    for cols in parts[1:]:
        with_left(cols)
    begin_early(1, mirror, second)
    tail_gram.wait_recv()
    reduced[:, 2 * NT:] = diag[0, :, 2 * NT:] - lgram[:, 2 * NT:] - came[0, :, 2 * NT:]
    row = lax.axis_index("col") * height + lax.broadcasted_iota(jnp.int32, (height, size), 0)
    col = lax.broadcasted_iota(jnp.int32, (height, size), 1)
    blocks[1] = jnp.where(col <= row, a_one[mine, :], 0.0)
    solved[0] = a_one[size:size + height, :]
    solved[1] = a_one[size + height:, :]

    def ready_two():
        second[mine, :] = mirror[...]
        a_two[size + height:, :] = mirror[...]
        over_upper.wait_recv()
        a_two[size:size + height, :] = first[mine, :]

    late = factor(1, a_two, reduced, mirror, second, first.at[mine], first, ready_two)

    zs = [split(z_ref[i * height:(i + 1) * height, :]) for i in range(2)]
    back = []
    for i, (full, by) in ((1, (second, 1)), (0, (first, -1))):
        if i == 0:
            gather_round(RELAY, 3, late)
        for n, cols in enumerate(parts):
            there = pl.ds(n * 2 * NT, 2 * NT)
            grams[i, :, cols] = dot3(zs[i], split(full[cols, :]), NTR)
            back.append(over(3 + 2 * n + i, by, grams.at[i, :, there], came.at[1 + i, :, there]))
            back[-1].start()
    for copy in (head_gram, tail_gram, over_upper):
        copy.wait_send()
    for copy in back:
        copy.wait()
    blocks[0] = reduced[...] - came[1] - came[2]


def solution(mesh):
    def shards(diag_blocks, left_blocks, right_blocks):
        height, size = left_blocks.shape[1:]
        part, full = (height, size), (size, size)
        tall = (size + 2 * height, size)
        shapes = [tall, tall, full, full, full, full, (2 * height, size), (size // NT, NT, NT)]
        shapes += [(NT, NT)] * 4 + [part] * 5 + [(3, *part), (2, *part)]
        sems = [pltpu.SemaphoreType.DMA((2, 5, SLOTS))] * 2 + [pltpu.SemaphoreType.DMA((16,))] * 2
        blocks, solved = pl.pallas_call(
            kernel,
            out_shape=[jax.ShapeDtypeStruct((2, *part), F32)] * 2,
            in_specs=[pl.BlockSpec(memory_space=pltpu.VMEM)] * 3,
            out_specs=[pl.BlockSpec(memory_space=pltpu.VMEM)] * 2,
            scratch_shapes=[pltpu.VMEM(s, F32) for s in shapes] + sems,
            compiler_params=pltpu.CompilerParams(
                vmem_limit_bytes=56 << 20, collective_id=0, has_side_effects=True
            ),
        )(diag_blocks, left_blocks[0], right_blocks[0])
        return blocks, solved[None]

    in_specs = (P("tm", "col", None), P("tm", "col", None), P("tm", "col", None))
    out_specs = (P("tm", "col", None), P("tm", None, "col", None))
    return jax.shard_map(shards, mesh=mesh, in_specs=in_specs, out_specs=out_specs, check_vma=False)
```
